256 devices in a mesh: grp: 4 (over y), tok: 64 (over x, z, core).
Axes of the slice: x: 4, y: 4, z: 8, core: 2. Of those that a mesh axis runs over, the one named last changes fastest.
Arguments:
- hidden_in: bfloat16 [4, 16384, 2048], P('grp', 'tok'), may hold values from -6 to 6
- doc_ids: int32 [4, 16384], P('grp', 'tok'), may hold values from 0 to 63, never falling along the last dimension, each value on 1 to 512 neighbouring positions
- prefix_kv: bfloat16 [4, 2048, 1024], P('grp', 'tok'), may hold values from -1024 to 1024
- prefix_owner: int32 [4], replicated, may hold values from 0 to 3, each once
- norm_gain: bfloat16 [2048], replicated, may hold values from 0.5 to 2
- query_gain: bfloat16 [128], replicated, may hold values from 0.59765625 to 2.390625
- key_norm_gain: bfloat16 [128], replicated, may hold values from 0.59765625 to 2.390625
- w_qkv: bfloat16 [2048, 2048], P('tok'), may hold values from -0.125 to 0.125
- w_out: bfloat16 [1024, 2048], P('tok'), may hold values from -0.1875 to 0.1875
Outputs:
- attn_out: bfloat16 [4, 16384, 2048], P('grp', 'tok')
- key_cache: bfloat16 [4, 16384, 512], P('grp', 'tok')
- value_cache: bfloat16 [4, 16384, 512], P('grp', 'tok')
The draws below stay inside these ranges and needn't reach their ends.
Inputs may be any that keep to these rules, and one draw needn't show every extreme that they name: `doc_ids`: in each group the ids never fall; every one of the 64 requests has 1 to 512 tokens, and one has exactly 512. `prefix_owner`: A permutation of the groups.
All inputs are finite; a program needn't handle non-finite values.
Results may differ from the reference program's by a relative error of at most 0.013.
The reference program's roundings to bfloat16 on the way count: a program that leaves them out, or rounds other values in their place, can miss the bound.
Values may be sent and summed in bfloat16 or wider, within the bound.
No kernel may reach another device: no remote copies, remote signals or barrier semaphores. Data moves between devices by JAX's collectives and lax.ppermute only.
A program may use at most 128 MiB of HBM per device.

```python
import math
import jax
import jax.numpy as jnp
import numpy as np
from jax import lax

D = 2048
QUERY_HEADS = 8
KEY_VALUE_HEADS = 4
HEAD_SIZE = 128
TOK_DEV = 256
GROUPS = 4
GROUP_TOKENS = 16384
PREFIX_TOKENS = 2048
MOST_SUFFIX = 512
REQ_ROW = 64
QKVW = 2048


def draw_prefix_kv(key, part):
    key_one, key_two = jax.random.split(jax.random.fold_in(key, 17), 2)
    half_width = KEY_VALUE_HEADS * HEAD_SIZE
    key_heads = jnp.clip(jax.random.normal(key_one, (GROUPS, PREFIX_TOKENS, half_width), jnp.float32), -5.0, 5.0)
    value_heads = jnp.clip(jax.random.normal(key_two, (GROUPS, PREFIX_TOKENS, half_width), jnp.float32), -5.0, 5.0)
    return jnp.concatenate([key_heads, value_heads], axis=-1).astype(jnp.bfloat16)


def shard_levels(key, shape, cuts, smallest, top_value):
    loudness, own = 1.0, jax.random.fold_in(key, 6)
    for axis_at, blocks in cuts:
        draws = jnp.exp(jax.random.uniform(jax.random.fold_in(own, axis_at), (blocks,), jnp.float32, smallest / len(cuts), top_value / len(cuts)))
        loudness = loudness * jnp.repeat(draws, shape[axis_at] // blocks).reshape([-1 if axis == axis_at else 1 for axis in range(len(shape))])
    return loudness


def split_up(number_of, total, limit, skew):
    portions = [(1 << 20) // math.isqrt(rank ** skew) + 1 for rank in range(2, number_of + 1)]
    rest, holding = total - limit - (number_of - 1), [1] * (number_of - 1)
    while rest > 0:
        free = [i for i in range(number_of - 1) if holding[i] < limit]
        pool, remaining = sum([portions[i] for i in free]), rest
        for i in free:
            addition = min(limit - holding[i], max(1, remaining * portions[i] // pool), rest)
            holding[i] = holding[i] + addition
            rest = rest - addition
    return np.array([limit] + holding)


def uneven(stream_key, number_of, total, reach, skew):
    if number_of == 2:
        one = jax.random.randint(stream_key, (), max(1, total - reach), min(reach, total - 1) + 1)
        return jnp.stack([one, total - one])
    tallies = jnp.asarray(split_up(number_of, total, reach, skew), jnp.int32)
    twos = (number_of - 1) // 2
    giver, sink = tallies[1:1 + 2 * twos:2], tallies[2:2 + 2 * twos:2]
    room = jnp.minimum(giver - 1, reach - sink)
    moved = jax.random.randint(jax.random.fold_in(stream_key, 1), (twos,), 0, 1 << 20) % (room + 1)
    tallies = tallies.at[1:1 + 2 * twos:2].set(giver - moved).at[2:2 + 2 * twos:2].set(sink + moved)
    return tallies[jax.random.permutation(jax.random.fold_in(stream_key, 2), number_of)]


def centred(rng, dims, width, limit, pieces=(), held_as=jnp.bfloat16):
    result = jax.random.normal(rng, dims, jnp.float32) * width
    if len(pieces) > 0:
        result = shard_levels(rng, dims, pieces, -0.22, 0.18) * result
    return jnp.clip(result, min=-limit, max=limit).astype(held_as)


def setup_inputs(seed: int = 0) -> dict:
    key_of = jax.random.split(jax.random.key(seed), 10)
    return {
        "hidden_in": centred(key_of[0], (GROUPS, GROUP_TOKENS, D), 1.0, 6.0, ((0, 4), (1, 64))),
        "doc_ids": jax.vmap(lambda own: jnp.searchsorted(jnp.cumsum(uneven(own, REQ_ROW, GROUP_TOKENS, MOST_SUFFIX, 2)), jnp.arange(GROUP_TOKENS), side="right"))(jax.random.split(key_of[1], GROUPS)).reshape((GROUPS, GROUP_TOKENS)).astype(jnp.int32),
        "prefix_kv": draw_prefix_kv(jax.random.fold_in(key_of[9], 71), 0),
        "prefix_owner": jax.random.permutation(key_of[3], GROUPS).astype(jnp.int32),
        "norm_gain": jnp.clip(jnp.exp(jax.random.uniform(key_of[4], (D,), jnp.float32, math.log(0.5), math.log(2.0))), 0.5, 2.0).astype(jnp.bfloat16),
        "query_gain": jnp.clip(jnp.exp(jax.random.uniform(key_of[5], (HEAD_SIZE,), jnp.float32, math.log(0.59765625), math.log(2.390625))), 0.59765625, 2.390625).astype(jnp.bfloat16),
        "key_norm_gain": jnp.clip(jnp.exp(jax.random.uniform(key_of[6], (HEAD_SIZE,), jnp.float32, math.log(0.59765625), math.log(2.390625))), 0.59765625, 2.390625).astype(jnp.bfloat16),
        "w_qkv": centred(key_of[7], (D, QKVW), D ** -0.5, 0.125, ((0, 64),)),
        "w_out": centred(key_of[8], (QUERY_HEADS * HEAD_SIZE, D), (QUERY_HEADS * HEAD_SIZE) ** -0.5, 0.1875, ((0, 64),)),
    }


epsilon = 1e-06
theta_base = 1000000.0
floor_score = -1e+30

def root_mean_scale(value_heads):
    return value_heads * lax.rsqrt(lax.optimization_barrier(jnp.mean(value_heads * value_heads, axis=-1, keepdims=True)) + epsilon)

def rotary_embed(heads, token_positions):
    half_width = heads.shape[-1] // 2
    freqs = theta_base ** (-jnp.arange(half_width, dtype=jnp.float32) / half_width)
    angles = token_positions[:, None] * freqs[None, :]
    cosine = jnp.cos(angles)[:, None, :]
    sine = jnp.sin(angles)[:, None, :]
    first = heads[..., :half_width]
    second = heads[..., half_width:]
    return jnp.concatenate([first * cosine - second * sine, second * cosine + first * sine], axis=-1)

def reference(hidden_in, doc_ids, prefix_kv, prefix_owner, norm_gain, query_gain, key_norm_gain, w_qkv, w_out):
    query_width = QUERY_HEADS * HEAD_SIZE
    key_value_width = KEY_VALUE_HEADS * HEAD_SIZE
    group_ratio = QUERY_HEADS // KEY_VALUE_HEADS
    scale = HEAD_SIZE ** (-0.5)
    outputs = []
    key_rows = []
    value_rows = []
    for group in range(GROUPS):
        tokens = hidden_in[group].astype(jnp.float32)
        normed = (root_mean_scale(tokens) * norm_gain.astype(jnp.float32)).astype(jnp.bfloat16)
        query_key_value = jnp.dot(normed, w_qkv, preferred_element_type=jnp.float32)
        ids = doc_ids[group]
        index = jnp.arange(GROUP_TOKENS, dtype=jnp.int32)
        changed = jnp.concatenate([jnp.ones((1,), dtype=jnp.bool_), ids[1:] != ids[:-1]])
        run_start = lax.cummax(jnp.where(changed, index, 0), axis=0)
        token_positions = (PREFIX_TOKENS + index - run_start).astype(jnp.float32)
        query_heads = rotary_embed(root_mean_scale(query_key_value[:, :query_width].reshape(GROUP_TOKENS, QUERY_HEADS, HEAD_SIZE)) * query_gain.astype(jnp.float32), token_positions).astype(jnp.bfloat16)
        key_heads = rotary_embed(root_mean_scale(query_key_value[:, query_width:query_width + key_value_width].reshape(GROUP_TOKENS, KEY_VALUE_HEADS, HEAD_SIZE)) * key_norm_gain.astype(jnp.float32), token_positions).astype(jnp.bfloat16)
        value_heads = query_key_value[:, query_width + key_value_width:].astype(jnp.bfloat16)
        key_flat = key_heads.reshape(GROUP_TOKENS, key_value_width)
        key_rows.append(key_flat)
        value_rows.append(value_heads)
        query_heads = lax.optimization_barrier(query_heads)
        key_heads = lax.optimization_barrier(key_heads)
        value_heads = lax.optimization_barrier(value_heads)
        owned_prefix = lax.dynamic_index_in_dim(prefix_kv, prefix_owner[group], 0, keepdims=False).astype(jnp.float32)
        cached_prefix_keys = owned_prefix[:, :key_value_width].reshape(PREFIX_TOKENS, KEY_VALUE_HEADS, HEAD_SIZE)
        cached_prefix_values = owned_prefix[:, key_value_width:].reshape(PREFIX_TOKENS, KEY_VALUE_HEADS, HEAD_SIZE)
        grouped_queries = query_heads.astype(jnp.float32).reshape(GROUP_TOKENS, KEY_VALUE_HEADS, group_ratio, HEAD_SIZE)
        padded_keys = jnp.concatenate([jnp.zeros((MOST_SUFFIX, KEY_VALUE_HEADS, HEAD_SIZE), jnp.float32), key_heads.astype(jnp.float32)], axis=0)
        padded_values = jnp.concatenate([jnp.zeros((MOST_SUFFIX, key_value_width), jnp.float32), value_heads.astype(jnp.float32)], axis=0).reshape(MOST_SUFFIX + GROUP_TOKENS, KEY_VALUE_HEADS, HEAD_SIZE)
        ids_pad = jnp.concatenate([jnp.full((MOST_SUFFIX,), -1, jnp.int32), ids])

        def block(number):
            start = number * TOK_DEV
            query_block = lax.dynamic_slice_in_dim(grouped_queries, start, TOK_DEV, 0)
            query_ids = lax.dynamic_slice_in_dim(ids, start, TOK_DEV, 0)
            near_keys = lax.dynamic_slice_in_dim(padded_keys, start, MOST_SUFFIX + TOK_DEV, 0)
            near_values = lax.dynamic_slice_in_dim(padded_values, start, MOST_SUFFIX + TOK_DEV, 0)
            near_ids = lax.dynamic_slice_in_dim(ids_pad, start, MOST_SUFFIX + TOK_DEV, 0)
            query_index = start + jnp.arange(TOK_DEV, dtype=jnp.int32)
            key_index = start - MOST_SUFFIX + jnp.arange(MOST_SUFFIX + TOK_DEV, dtype=jnp.int32)
            allowed = (query_ids[:, None] == near_ids[None, :]) & (key_index[None, :] <= query_index[:, None])
            far = jnp.einsum('rgjd,kgd->gjrk', query_block, cached_prefix_keys) * scale
            near = jnp.einsum('rgjd,kgd->gjrk', query_block, near_keys) * scale
            near = jnp.where(allowed[None, None], near, floor_score)
            top = jnp.maximum(lax.optimization_barrier(jnp.max(far, axis=-1)), lax.optimization_barrier(jnp.max(near, axis=-1)))
            far_weights = jnp.exp(far - top[..., None])
            near_weights = jnp.where(allowed[None, None], jnp.exp(near - top[..., None]), 0.0)
            total = lax.optimization_barrier(jnp.sum(far_weights, axis=-1)) + lax.optimization_barrier(jnp.sum(near_weights, axis=-1))
            far_rounded = lax.optimization_barrier(far_weights.astype(jnp.bfloat16)).astype(jnp.float32)
            near_rounded = lax.optimization_barrier(near_weights.astype(jnp.bfloat16)).astype(jnp.float32)
            mixed = jnp.einsum('gjrk,kgd->gjrd', far_rounded, cached_prefix_values) + jnp.einsum('gjrk,kgd->gjrd', near_rounded, near_values)
            attended = mixed / total[..., None]
            return jnp.transpose(attended, (2, 0, 1, 3)).reshape(TOK_DEV, query_width).astype(jnp.bfloat16)
        blocks = lax.map(block, jnp.arange(GROUP_TOKENS // TOK_DEV, dtype=jnp.int32))
        attended = blocks.reshape(GROUP_TOKENS, query_width)
        outputs.append(jnp.dot(attended, w_out, preferred_element_type=jnp.float32).astype(jnp.bfloat16))
    return (jnp.stack(outputs), jnp.stack(key_rows), jnp.stack(value_rows))
```

```python
import functools
import math

import jax
import jax.numpy as jnp
from jax import lax
from jax.experimental import pallas as pl
from jax.experimental.pallas import tpu as pltpu
from jax.sharding import PartitionSpec as P

NX, NZ, NC, NY = 4, 8, 2, 4

epsilon = 1e-06
theta_base = 1000000.0
floor_score = -1e30
VMEM_LIMIT = 56 * 1024 * 1024


def place(x, z, c):
    return (x * NZ + z) * NC + c


def from_tok(block, dx=0, dz=0, dc=0):
    route = [
        (place((x + dx) % NX, (z + dz) % NZ, (c + dc) % NC), place(x, z, c))
        for x in range(NX)
        for z in range(NZ)
        for c in range(NC)
    ]
    return lax.ppermute(block, "tok", route)


def from_grp(block, dy):
    return lax.ppermute(block, "grp", [((y + dy) % NY, y) for y in range(NY)])


def from_previous_chip(block):
    chips = NX * NZ
    route = [(p * NC + c, (p + 1) * NC + c) for p in range(chips - 1) for c in range(NC)]
    return lax.ppermute(block, "tok", route)


def in_core_order(core, mine, other, axis):
    first = jnp.where(core == 0, mine, other)
    second = jnp.where(core == 0, other, mine)
    return jnp.concatenate([first, second], axis=axis)


def norm_kernel(x_ref, own_ref, peer_ref, gain_ref, np_ref, nq_ref, scratch):
    half = own_ref.shape[0]
    gain = gain_ref[...].astype(jnp.float32)
    x = x_ref[0]
    for part, ref in enumerate((own_ref, peer_ref)):
        tokens = ref[...].astype(jnp.float32)
        mean = jnp.mean(tokens * tokens, axis=-1, keepdims=True)
        scratch[...] = (tokens * lax.rsqrt(mean + epsilon) * gain).astype(jnp.bfloat16)
        for j in range(NX):
            at = pl.multiple_of(((x + j) % NX) * 512, 512)
            np_ref[pl.ds(part * half, half), j * 256 : (j + 1) * 256] = scratch[:, pl.ds(at, 256)]
            at = pl.multiple_of(((x + j) % NX) * 512 + 256, 256)
            nq_ref[pl.ds(part * half, half), j * 256 : (j + 1) * 256] = scratch[:, pl.ds(at, 256)]


def input_norm(x, own, peer, gain):
    rows, width = own.shape
    out = jax.ShapeDtypeStruct((2 * rows, width // 2), jnp.bfloat16)
    vmem = pl.BlockSpec(memory_space=pltpu.VMEM)
    return pl.pallas_call(
        norm_kernel,
        out_shape=(out, out),
        in_specs=[pl.BlockSpec(memory_space=pltpu.SMEM), vmem, vmem, vmem],
        out_specs=(vmem, vmem),
        scratch_shapes=[pltpu.VMEM((rows, width), jnp.bfloat16)],
        compiler_params=pltpu.CompilerParams(vmem_limit_bytes=VMEM_LIMIT),
        name="input_norm",
    )(x, own, peer, gain)


def qkv_kernel(
    y_ref, np_ref, nq_ref, p0, p1, p2, p3, q0, q1, q2, q3, cos_ref, sin_ref, qg_ref, kg_ref,
    out_ref, acc
):
    step = pl.program_id(0)
    block = (y_ref[0] + step) % NY
    for k, p in enumerate((p0, p1, p2, p3)):

        @pl.when(step == k)
        def _(p=p, k=k):
            total = jnp.dot(np_ref[...], p[...], preferred_element_type=jnp.float32)
            for j, q in enumerate((q0, q1, q2, q3)):
                total = total + jnp.dot(
                    nq_ref[:, j * 256 : (j + 1) * 256],
                    q[k * 256 : (k + 1) * 256, :],
                    preferred_element_type=jnp.float32,
                )
            acc[...] = total

    @pl.when(block == 3)
    def _():
        out_ref[0] = acc[...].astype(jnp.bfloat16)

    @pl.when(block < 3)
    def _():
        gain = jnp.where(block == 2, kg_ref[...].astype(jnp.float32), qg_ref[...].astype(jnp.float32))
        for h in range(2):
            a = acc[:, h * 128 : (h + 1) * 128]
            mean = jnp.mean(a * a, axis=-1, keepdims=True)
            a = a * lax.rsqrt(mean + epsilon) * gain
            turned = a * cos_ref[...] + pltpu.roll(a, 64, 1) * sin_ref[...]
            out_ref[0, :, h * 128 : (h + 1) * 128] = turned.astype(jnp.bfloat16)


def joint_projection(y, normed_p, normed_q, p, q, cosine, sine, query_gain, key_gain):
    rows = normed_p.shape[0]
    whole = lambda a: pl.BlockSpec(a.shape, lambda i, y_ref: (0,) * a.ndim)
    args = [normed_p, normed_q, *p, *q, cosine, sine, query_gain, key_gain]
    return pl.pallas_call(
        qkv_kernel,
        out_shape=jax.ShapeDtypeStruct((NY, rows, 256), jnp.bfloat16),
        grid_spec=pltpu.PrefetchScalarGridSpec(
            num_scalar_prefetch=1,
            grid=(NY,),
            in_specs=[whole(a) for a in args],
            out_specs=pl.BlockSpec((1, rows, 256), lambda i, y_ref: ((y_ref[0] + i) % NY, 0, 0)),
            scratch_shapes=[pltpu.VMEM((rows, 256), jnp.float32)],
        ),
        compiler_params=pltpu.CompilerParams(
            dimension_semantics=("arbitrary",), vmem_limit_bytes=VMEM_LIMIT
        ),
        cost_estimate=pl.CostEstimate(
            flops=2 * rows * 2048 * 1024, transcendentals=0, bytes_accessed=8 << 20
        ),
        name="joint_projection",
    )(y, *args)


LANES = (((1,), (1,)), ((), ()))


def prefix_kernel(scale, qkv_ref, *refs):
    *pieces, acc_ref, top_ref, total_ref = refs
    for h in range(4):
        g = h // 2
        q = qkv_ref[g, :, (h % 2) * 128 : (h % 2 + 1) * 128]
        scores = [
            lax.dot_general(
                q, r[:, g * 128 : (g + 1) * 128], LANES, preferred_element_type=jnp.float32
            )
            for r in pieces
        ]
        top = functools.reduce(
            jnp.maximum, [jnp.max(s, axis=-1, keepdims=True) for s in scores]
        )
        total = jnp.zeros_like(top)
        acc = jnp.zeros((q.shape[0], 128), jnp.float32)
        for s, r in zip(scores, pieces):
            w = jnp.exp2((s - top) * scale)
            total = total + jnp.sum(w, axis=-1, keepdims=True)
            acc = acc + jnp.dot(
                w.astype(jnp.bfloat16),
                r[:, 256 + g * 128 : 256 + (g + 1) * 128],
                preferred_element_type=jnp.float32,
            )
        acc_ref[h] = acc
        top_ref[h] = top
        total_ref[h] = total


def prefix_attention(qkv, pieces, scale, block_rows=128):
    rows = qkv.shape[1]
    stat = jax.ShapeDtypeStruct((4, rows, 1), jnp.float32)
    stat_spec = pl.BlockSpec((4, block_rows, 1), lambda i: (0, i, 0))
    keys = sum(p.shape[0] for p in pieces)
    return pl.pallas_call(
        functools.partial(prefix_kernel, scale),
        out_shape=(jax.ShapeDtypeStruct((4, rows, 128), jnp.float32), stat, stat),
        grid=(rows // block_rows,),
        in_specs=[pl.BlockSpec((2, block_rows, 256), lambda i: (0, i, 0))]
        + [pl.BlockSpec(p.shape, lambda i: (0, 0)) for p in pieces],
        out_specs=(pl.BlockSpec((4, block_rows, 128), lambda i: (0, i, 0)), stat_spec, stat_spec),
        compiler_params=pltpu.CompilerParams(
            dimension_semantics=("arbitrary",), vmem_limit_bytes=VMEM_LIMIT
        ),
        cost_estimate=pl.CostEstimate(
            flops=4 * 4 * rows * keys * 128, transcendentals=4 * rows * keys, bytes_accessed=4 << 20
        ),
        name="prefix_attention",
    )(qkv, *pieces)


def suffix_kernel(
    scale, qkv_ref, all_ref, halo_ref, acc_ref, top_ref, total_ref, qm_ref, qi_ref, km_ref, ki_ref,
    out_ref
):
    chip = all_ref.shape[1]
    allowed = (qm_ref[...] == km_ref[...]) & (ki_ref[...] <= qi_ref[...])
    for h in range(4):
        g = h // 2
        at = slice(g * 128, (g + 1) * 128)
        q = qkv_ref[g, :, (h % 2) * 128 : (h % 2 + 1) * 128]
        keys = (halo_ref[0, :, at], all_ref[2, :, at])
        values = (halo_ref[1, :, at], all_ref[3, :, at])
        scores = [
            jnp.where(
                allowed[:, i * chip : (i + 1) * chip],
                lax.dot_general(q, k, LANES, preferred_element_type=jnp.float32),
                floor_score,
            )
            for i, k in enumerate(keys)
        ]
        before = top_ref[h]
        top = jnp.maximum(
            before,
            jnp.maximum(*[jnp.max(s, axis=-1, keepdims=True) for s in scores]),
        )
        shrink = jnp.exp2((before - top) * scale)
        total = total_ref[h] * shrink
        acc = acc_ref[h] * shrink
        for s, v in zip(scores, values):
            w = jnp.exp2((s - top) * scale)
            total = total + jnp.sum(w, axis=-1, keepdims=True)
            acc = acc + jnp.dot(w.astype(jnp.bfloat16), v, preferred_element_type=jnp.float32)
        out_ref[:, h * 128 : (h + 1) * 128] = (acc / total).astype(jnp.bfloat16)


def suffix_attention(qkv, halo, partial, marks_q, index_q, marks_k, index_k, scale, block_rows=128):
    rows = qkv.shape[1]
    stat_spec = pl.BlockSpec((4, block_rows, 1), lambda i: (0, i, 0))
    meta = pl.BlockSpec((block_rows, 1), lambda i: (i, 0))
    return pl.pallas_call(
        functools.partial(suffix_kernel, scale),
        out_shape=jax.ShapeDtypeStruct((rows, 512), jnp.bfloat16),
        grid=(rows // block_rows,),
        in_specs=[
            pl.BlockSpec((2, block_rows, 256), lambda i: (0, i, 0)),
            pl.BlockSpec(qkv.shape, lambda i: (0, 0, 0)),
            pl.BlockSpec(halo.shape, lambda i: (0, 0, 0)),
            pl.BlockSpec((4, block_rows, 128), lambda i: (0, i, 0)),
            stat_spec,
            stat_spec,
            meta,
            meta,
            pl.BlockSpec(marks_k.shape, lambda i: (0, 0)),
            pl.BlockSpec(index_k.shape, lambda i: (0, 0)),
        ],
        out_specs=pl.BlockSpec((block_rows, 512), lambda i: (i, 0)),
        compiler_params=pltpu.CompilerParams(
            dimension_semantics=("arbitrary",), vmem_limit_bytes=VMEM_LIMIT
        ),
        cost_estimate=pl.CostEstimate(
            flops=4 * 4 * rows * 1024 * 128, transcendentals=4 * rows * 1024, bytes_accessed=4 << 20
        ),
        name="suffix_attention",
    )(qkv, qkv, halo, *partial, marks_q, index_q, marks_k, index_k)


def gather_projection(w, x, y, z, core):
    def columns(c):
        start = jnp.where(y < 2, 512 * c + 256 * y, 512 * y + 256 * c)
        return lax.dynamic_slice(w, (jnp.int32(0), start), (w.shape[0], 256))

    mine = columns(core)
    other = from_tok(columns(1 - core), dc=1)
    unit = in_core_order(core, mine, other, 0)
    ring = jnp.concatenate([unit] + [from_tok(unit, dz=d) for d in range(1, NZ)], axis=0)
    unit_rows = unit.shape[0]
    strip = lax.dynamic_slice_in_dim(
        jnp.concatenate([ring, ring], axis=0), ((NZ - z) % NZ) * unit_rows, NZ * unit_rows, 0
    )
    half = strip.shape[0] // 2
    p, q = strip[:half], strip[half:]
    p = jnp.concatenate([p] + [from_tok(p, dx=d) for d in range(1, NX)], axis=0)
    q = jnp.concatenate([q] + [from_grp(q, d) for d in range(1, NY)], axis=0)
    return (
        [p] + [from_grp(p, d) for d in range(1, NY)],
        [q] + [from_tok(q, dx=d) for d in range(1, NX)],
    )


def gather_prefix(block, owner, y, core):
    owners = jnp.stack([block] + [from_grp(block, d) for d in range(1, NY)])
    rows = lax.dynamic_index_in_dim(owners, (owner - y) % NY, 0, keepdims=False)
    width = rows.shape[1] // 2

    def heads(c):
        return jnp.concatenate(
            [
                lax.dynamic_slice_in_dim(rows, c * (width // 2), width // 2, 1),
                lax.dynamic_slice_in_dim(rows, width + c * (width // 2), width // 2, 1),
            ],
            axis=1,
        )

    unit = jnp.concatenate([heads(core), from_tok(heads(1 - core), dc=1)], axis=0)
    strip = jnp.concatenate([unit] + [from_tok(unit, dx=d) for d in range(1, NX)], axis=0)
    pieces = [strip]
    up, down = strip, strip
    for _ in range(3):
        up, down = from_tok(up, dz=-1), from_tok(down, dz=1)
        pieces += [up, down]
    half = strip.shape[0] // 2
    return pieces + [from_tok(up[:half], dz=-1), from_tok(down[half:], dz=1)]


def per_device(
    hidden_in, doc_ids, prefix_kv, prefix_owner, norm_gain, query_gain, key_norm_gain, w_qkv, w_out
):
    rows = hidden_in.shape[1]
    head_dim = query_gain.shape[0]
    prefix_len = prefix_kv.shape[1] * lax.axis_size("tok")
    scale = head_dim ** (-0.5) * math.log2(math.e)
    place_tok = lax.axis_index("tok")
    y = lax.axis_index("grp")
    x, z, core = place_tok // (NZ * NC), (place_tok // NC) % NZ, place_tok % NC

    out_weights = lax.all_gather(w_out, "tok", axis=0, tiled=True)

    own = hidden_in[0]
    peer = from_tok(own, dc=1)
    marks = doc_ids[0] + 1
    marks_chip = jnp.concatenate([marks, from_tok(marks, dc=1)])
    marks_before = from_previous_chip(marks_chip)
    index = jnp.arange(rows, dtype=jnp.int32)
    index_chip = jnp.concatenate([index + core * rows, index + (1 - core) * rows])
    marks_k = jnp.concatenate([marks_before, marks_chip])[None, :]
    index_k = jnp.concatenate([jnp.full((2 * rows,), -1, jnp.int32), index_chip])[None, :]
    marks_q, index_q = marks_chip[:, None], index_chip[:, None]
    earlier = (marks_q == marks_k) & (index_k < index_q)
    offset = jnp.sum(earlier.astype(jnp.int32), axis=1)
    token_positions = (prefix_len + offset).astype(jnp.float32)
    half_width = head_dim // 2
    freqs = theta_base ** (-jnp.arange(half_width, dtype=jnp.float32) / half_width)
    angles = token_positions[:, None] * freqs[None, :]
    cosine, sine = jnp.cos(angles), jnp.sin(angles)
    cosine = jnp.concatenate([cosine, cosine], axis=1)
    sine = jnp.concatenate([-sine, sine], axis=1)

    p, q = gather_projection(w_qkv, x, y, z, core)
    pieces = gather_prefix(prefix_kv[0], prefix_owner[y], y, core)
    normed_p, normed_q = input_norm(x[None], own, peer, norm_gain[None, :])
    qkv = joint_projection(
        y[None], normed_p, normed_q, p, q, cosine, sine, query_gain[None, :], key_norm_gain[None, :]
    )
    halo = from_previous_chip(qkv[2:])
    partial = prefix_attention(qkv, pieces, scale)
    attended = suffix_attention(qkv, halo, partial, marks_q, index_q, marks_k, index_k, scale)
    attended = in_core_order(core, attended[:rows], from_tok(attended[rows:], dc=1), 1)
    projected = jnp.dot(attended, out_weights, preferred_element_type=jnp.float32)

    kv_got = from_tok(qkv[2:, rows:], dc=1)
    cache = in_core_order(core, qkv[2:, :rows], kv_got, 2)
    return (projected.astype(jnp.bfloat16)[None], cache[0][None], cache[1][None])


def solution(mesh):
    return jax.shard_map(
        per_device,
        mesh=mesh,
        in_specs=(
            P("grp", "tok", None),
            P("grp", "tok"),
            P("grp", "tok", None),
            P(),
            P(),
            P(),
            P(),
            P("tok", None),
            P("tok", None),
        ),
        out_specs=(P("grp", "tok", None), P("grp", "tok", None), P("grp", "tok", None)),
        check_vma=False,
    )
```

```python
import functools
import math

import jax
import jax.numpy as jnp
from jax import lax
from jax.experimental import pallas as pl
from jax.experimental.pallas import tpu as pltpu
from jax.sharding import PartitionSpec as P

NX, NZ, NC, NY = 4, 8, 2, 4

epsilon = 1e-06
theta_base = 1000000.0
floor_score = -1e30
VMEM_LIMIT = 56 * 1024 * 1024


def place(x, z, c):
    return (x * NZ + z) * NC + c


def from_tok(block, dx=0, dz=0, dc=0):
    route = [
        (place((x + dx) % NX, (z + dz) % NZ, (c + dc) % NC), place(x, z, c))
        for x in range(NX)
        for z in range(NZ)
        for c in range(NC)
    ]
    return lax.ppermute(block, "tok", route)


def from_grp(block, dy):
    return lax.ppermute(block, "grp", [((y + dy) % NY, y) for y in range(NY)])


def from_previous_chip(block):
    chips = NX * NZ
    route = [(p * NC + c, (p + 1) * NC + c) for p in range(chips - 1) for c in range(NC)]
    return lax.ppermute(block, "tok", route)


def in_core_order(core, mine, other, axis):
    first = jnp.where(core == 0, mine, other)
    second = jnp.where(core == 0, other, mine)
    return jnp.concatenate([first, second], axis=axis)


def norm_kernel(x_ref, own_ref, peer_ref, gain_ref, np_ref, nq_ref, scratch):
    half = own_ref.shape[0]
    gain = gain_ref[...].astype(jnp.float32)
    x = x_ref[0]
    for part, ref in enumerate((own_ref, peer_ref)):
        tokens = ref[...].astype(jnp.float32)
        mean = jnp.mean(tokens * tokens, axis=-1, keepdims=True)
        scratch[...] = (tokens * lax.rsqrt(mean + epsilon) * gain).astype(jnp.bfloat16)
        for j in range(NX):
            at = pl.multiple_of(((x + j) % NX) * 512, 512)
            np_ref[pl.ds(part * half, half), j * 256 : (j + 1) * 256] = scratch[:, pl.ds(at, 256)]
            at = pl.multiple_of(((x + j) % NX) * 512 + 256, 256)
            nq_ref[pl.ds(part * half, half), j * 256 : (j + 1) * 256] = scratch[:, pl.ds(at, 256)]


def input_norm(x, own, peer, gain):
    rows, width = own.shape
    out = jax.ShapeDtypeStruct((2 * rows, width // 2), jnp.bfloat16)
    vmem = pl.BlockSpec(memory_space=pltpu.VMEM)
    return pl.pallas_call(
        norm_kernel,
        out_shape=(out, out),
        in_specs=[pl.BlockSpec(memory_space=pltpu.SMEM), vmem, vmem, vmem],
        out_specs=(vmem, vmem),
        scratch_shapes=[pltpu.VMEM((rows, width), jnp.bfloat16)],
        compiler_params=pltpu.CompilerParams(vmem_limit_bytes=VMEM_LIMIT),
        name="input_norm",
    )(x, own, peer, gain)


def qkv_kernel(
    y_ref, np_ref, nq_ref, p0, p1, p2a, p2b, p3, q0, q1, q2a, q2b, q3, cos_ref, sin_ref, qg_ref, kg_ref,
    out_ref, acc
):
    step = pl.program_id(0)
    block = (y_ref[0] + step) % NY

    def add_p(total, piece, first):
        for j in range(piece.shape[0] // 384):
            total = total + jnp.dot(
                np_ref[:, (first + j) * 256 : (first + j + 1) * 256],
                piece[j * 384 : j * 384 + 256, :],
                preferred_element_type=jnp.float32,
            )
        return total

    def part_q(step):
        total = jnp.zeros(acc.shape, jnp.float32)
        for j, (q, k) in enumerate(((q0, step), (q1, step), (None, step), (q3, step))):
            if q is None:
                q, k = (q2a, step) if step < 2 else (q2b, step - 2)
            total = total + jnp.dot(
                nq_ref[:, j * 256 : (j + 1) * 256],
                q[k * 384 : k * 384 + 256, :],
                preferred_element_type=jnp.float32,
            )
        return total

    for k, ps in enumerate((((p0, 0),), ((p1, 0),), ((p2a, 0), (p2b, 2)), ((p3, 0),))):

        @pl.when(step == k)
        def _(ps=ps, k=k):
            total = part_q(k)
            for piece, first in ps:
                total = add_p(total, piece, first)
            acc[...] = total

    @pl.when(block == 3)
    def _():
        out_ref[0] = acc[...].astype(jnp.bfloat16)

    @pl.when(block < 3)
    def _():
        gain = jnp.where(block == 2, kg_ref[...].astype(jnp.float32), qg_ref[...].astype(jnp.float32))
        for h in range(2):
            a = acc[:, h * 128 : (h + 1) * 128]
            mean = jnp.mean(a * a, axis=-1, keepdims=True)
            a = a * lax.rsqrt(mean + epsilon) * gain
            turned = a * cos_ref[...] + pltpu.roll(a, 64, 1) * sin_ref[...]
            out_ref[0, :, h * 128 : (h + 1) * 128] = turned.astype(jnp.bfloat16)


def joint_projection(y, normed_p, normed_q, p, q, cosine, sine, query_gain, key_gain):
    rows = normed_p.shape[0]
    whole = lambda a: pl.BlockSpec(a.shape, lambda i, y_ref: (0,) * a.ndim)
    args = [normed_p, normed_q, *p, *q, cosine, sine, query_gain, key_gain]
    return pl.pallas_call(
        qkv_kernel,
        out_shape=jax.ShapeDtypeStruct((NY, rows, 256), jnp.bfloat16),
        grid_spec=pltpu.PrefetchScalarGridSpec(
            num_scalar_prefetch=1,
            grid=(NY,),
            in_specs=[whole(a) for a in args],
            out_specs=pl.BlockSpec((1, rows, 256), lambda i, y_ref: ((y_ref[0] + i) % NY, 0, 0)),
            scratch_shapes=[pltpu.VMEM((rows, 256), jnp.float32)],
        ),
        compiler_params=pltpu.CompilerParams(
            dimension_semantics=("arbitrary",), vmem_limit_bytes=VMEM_LIMIT
        ),
        cost_estimate=pl.CostEstimate(
            flops=2 * rows * 2048 * 1024, transcendentals=0, bytes_accessed=8 << 20
        ),
        name="joint_projection",
    )(y, *args)


LANES = (((1,), (1,)), ((), ()))


def suffix_kernel(
    scale, q_ref, ko_ref, vo_ref, kh_ref, vh_ref, qm_ref, qi_ref, km_ref, ki_ref,
    acc_ref, top_ref, total_ref, bias
):
    chip = ko_ref.shape[1]

    @pl.when(pl.program_id(0) == 0)
    def _():
        allowed = (qm_ref[...] == km_ref[...]) & (ki_ref[...] <= qi_ref[...])
        bias[...] = jnp.where(allowed, 0.0, floor_score)

    q = q_ref[0]
    scores = [
        lax.dot_general(q, k[0], LANES, preferred_element_type=jnp.float32)
        + bias[:, i * chip : (i + 1) * chip]
        for i, k in enumerate((kh_ref, ko_ref))
    ]
    top = jnp.maximum(*[jnp.max(s, axis=-1, keepdims=True) for s in scores])
    total = jnp.zeros_like(top)
    acc = jnp.zeros((q.shape[0], q.shape[1]), jnp.float32)
    for s, v in zip(scores, (vh_ref, vo_ref)):
        w = jnp.exp2((s - top) * scale)
        total = total + jnp.sum(w, axis=-1, keepdims=True)
        acc = acc + jnp.dot(w.astype(jnp.bfloat16), v[0], preferred_element_type=jnp.float32)
    acc_ref[0] = acc
    top_ref[0] = top
    total_ref[0] = total


def suffix_attention(qkv, halo, marks_q, index_q, marks_k, index_k, scale):
    rows = qkv.shape[1]
    stat = jax.ShapeDtypeStruct((4, rows, 1), jnp.float32)
    per_head = lambda width: pl.BlockSpec((1, rows, width), lambda h: (h, 0, 0))
    head = lambda block: pl.BlockSpec((1, rows, 128), lambda h: (block, 0, h // 2))
    whole = lambda a: pl.BlockSpec(a.shape, lambda h: (0, 0))
    return pl.pallas_call(
        functools.partial(suffix_kernel, scale),
        out_shape=(jax.ShapeDtypeStruct((4, rows, 128), jnp.float32), stat, stat),
        grid=(4,),
        in_specs=[
            pl.BlockSpec((1, rows, 128), lambda h: (h // 2, 0, h % 2)),
            head(2),
            head(3),
            head(0),
            head(1),
            whole(marks_q),
            whole(index_q),
            whole(marks_k),
            whole(index_k),
        ],
        out_specs=(per_head(128), per_head(1), per_head(1)),
        scratch_shapes=[pltpu.VMEM((rows, 2 * rows), jnp.float32)],
        compiler_params=pltpu.CompilerParams(
            dimension_semantics=("arbitrary",), vmem_limit_bytes=VMEM_LIMIT
        ),
        cost_estimate=pl.CostEstimate(
            flops=4 * 4 * rows * 1024 * 128, transcendentals=4 * rows * 1024, bytes_accessed=4 << 20
        ),
        name="suffix_attention",
    )(qkv, qkv, qkv, halo, halo, marks_q, index_q, marks_k, index_k)


def prefix_kernel(scale, core_ref, q_ref, k_ref, v_ref, acc_ref, top_ref, total_ref, out_ref):
    q = q_ref[0]
    step = 512
    starts = range(0, k_ref.shape[0], step)
    scores = [
        lax.dot_general(q, k_ref[i : i + step, :], LANES, preferred_element_type=jnp.float32)
        for i in starts
    ]
    before = top_ref[0]
    top = functools.reduce(
        jnp.maximum, [jnp.max(s, axis=-1, keepdims=True) for s in scores], before
    )
    shrink = jnp.exp2((before - top) * scale)
    total = total_ref[0] * shrink
    acc = acc_ref[0] * shrink
    for s, i in zip(scores, starts):
        w = jnp.exp2((s - top) * scale)
        total = total + jnp.sum(w, axis=-1, keepdims=True)
        acc = acc + jnp.dot(
            w.astype(jnp.bfloat16), v_ref[i : i + step, :], preferred_element_type=jnp.float32
        )
    out_ref[...] = (acc / total).astype(jnp.bfloat16)


def prefix_attention(core, qkv, prefix, suffix, scale):
    rows = qkv.shape[1]
    keys = prefix.shape[0]
    per_head = lambda width: pl.BlockSpec((1, rows, width), lambda h, c: (h, 0, 0))
    return pl.pallas_call(
        functools.partial(prefix_kernel, scale),
        out_shape=jax.ShapeDtypeStruct((rows, 512), jnp.bfloat16),
        grid_spec=pltpu.PrefetchScalarGridSpec(
            num_scalar_prefetch=1,
            grid=(4,),
            in_specs=[
                pl.BlockSpec((1, rows, 128), lambda h, c: (h // 2, 0, h % 2)),
                pl.BlockSpec((keys, 128), lambda h, c: (0, 2 * c[0] + h // 2)),
                pl.BlockSpec((keys, 128), lambda h, c: (0, 4 + 2 * c[0] + h // 2)),
                per_head(128),
                per_head(1),
                per_head(1),
            ],
            out_specs=pl.BlockSpec((rows, 128), lambda h, c: (0, h)),
        ),
        compiler_params=pltpu.CompilerParams(
            dimension_semantics=("arbitrary",), vmem_limit_bytes=VMEM_LIMIT
        ),
        cost_estimate=pl.CostEstimate(
            flops=4 * 4 * rows * keys * 128, transcendentals=4 * rows * keys, bytes_accessed=4 << 20
        ),
        name="prefix_attention",
    )(core, qkv, prefix, prefix, *suffix)


def out_kernel(place_ref, mine_ref, other_ref, w_ref, wo_ref, out_ref, heads, ordered):
    x, core = place_ref[0], place_ref[2]

    @pl.when(pl.program_id(0) == 0)
    def _():
        heads[:, pl.ds(pl.multiple_of(core * 512, 512), 512)] = mine_ref[...]
        heads[:, pl.ds(pl.multiple_of((1 - core) * 512, 512), 512)] = other_ref[...]
        for part in range(2):
            for j in range(NX):
                at = pl.multiple_of(((x + j) % NX) * 256 + part * 128, 128)
                to = part * 512 + j * 128
                ordered[:, to : to + 128] = heads[:, pl.ds(at, 128)]

    for w, c in ((w_ref, core), (wo_ref, 1 - core)):
        out_ref[:, pl.ds(pl.multiple_of(c * 256, 256), 256)] = jnp.dot(
            ordered[...], w[0], preferred_element_type=jnp.float32
        ).astype(jnp.bfloat16)


def output_projection(place_xyc, mine, other, w, w_other):
    rows = mine.shape[0]
    block = pl.BlockSpec((1, 1024, 256), lambda i, p: (i, 0, 0))
    half = pl.BlockSpec(mine.shape, lambda i, p: (0, 0))
    return pl.pallas_call(
        out_kernel,
        out_shape=jax.ShapeDtypeStruct((rows, 2048), jnp.bfloat16),
        grid_spec=pltpu.PrefetchScalarGridSpec(
            num_scalar_prefetch=1,
            grid=(NY,),
            in_specs=[half, half, block, block],
            out_specs=pl.BlockSpec((rows, 512), lambda i, p: (0, (p[1] + i) % NY)),
            scratch_shapes=[pltpu.VMEM((rows, 1024), jnp.bfloat16)] * 2,
        ),
        compiler_params=pltpu.CompilerParams(
            dimension_semantics=("arbitrary",), vmem_limit_bytes=VMEM_LIMIT
        ),
        cost_estimate=pl.CostEstimate(
            flops=2 * rows * 1024 * 2048, transcendentals=0, bytes_accessed=6 << 20
        ),
        name="output_projection",
    )(place_xyc, mine, other, w, w_other)


GROUP_ZC = [[place(x, z, c) for z in range(NZ) for c in range(NC)] for x in range(NX)]


def per_device(
    hidden_in, doc_ids, prefix_kv, prefix_owner, norm_gain, query_gain, key_norm_gain, w_qkv, w_out
):
    rows = hidden_in.shape[1]
    head_dim = query_gain.shape[0]
    prefix_len = prefix_kv.shape[1] * lax.axis_size("tok")
    scale = head_dim ** (-0.5) * math.log2(math.e)
    place_tok = lax.axis_index("tok")
    y = lax.axis_index("grp")
    x, core = place_tok // (NZ * NC), place_tok % NC

    own = hidden_in[0]
    marks = doc_ids[0] + 1
    prefix_rows = [prefix_kv[0]] + [from_grp(prefix_kv[0], d) for d in range(1, NY)]
    peer = from_tok(own, dc=1)
    marks_peer = from_tok(marks, dc=1)

    def columns(c):
        start = jnp.where(y < 2, 512 * c + 256 * y, 512 * y + 256 * c)
        return lax.dynamic_slice(w_qkv, (jnp.int32(0), start), (w_qkv.shape[0], 256))

    qkv_part = jnp.concatenate([columns(0), columns(1)], axis=1)
    out_part = lax.dynamic_slice(w_out, (jnp.int32(0), 512 * y), (w_out.shape[0], 512))
    both = lax.all_gather(
        jnp.concatenate([qkv_part, out_part], axis=0), "tok", axis_index_groups=GROUP_ZC
    )
    both, peer, marks_peer, prefix_rows = lax.optimization_barrier(
        (both, peer, marks_peer, prefix_rows)
    )

    both = lax.dynamic_slice_in_dim(both, core * 256, 256, 2)
    qkv_strip = both[:, :32].reshape(512, 256)
    out_strip = both[:, 32:].reshape(256, 256)
    mine = lax.dynamic_index_in_dim(
        jnp.stack(prefix_rows), (prefix_owner[y] - y) % NY, 0, keepdims=False
    )
    p_own = jnp.concatenate(
        [qkv_strip[:256], out_strip[:128]] + [mine[:, i * 256 : (i + 1) * 256] for i in range(4)]
    )
    q_own = jnp.concatenate([qkv_strip[256:], out_strip[128:]])
    p_all = [p_own] + [from_tok(p_own, dx=d) for d in range(1, NX)]
    q_all = [q_own] + [from_grp(q_own, d) for d in range(1, NY)]
    marks_chip = jnp.concatenate([marks, marks_peer])
    p_all, q_all = lax.optimization_barrier((p_all, q_all))
    prefix_part = jnp.concatenate(
        [
            jnp.concatenate([p[384 + 32 * i : 416 + 32 * i] for i in range(4)], axis=1)
            for p in p_all
        ]
    )
    prefix = lax.all_gather(prefix_part, "tok", axis_index_groups=GROUP_ZC, tiled=True)

    p0 = jnp.concatenate([p[:384] for p in p_all])
    q0 = jnp.concatenate(q_all)
    half = p0.shape[0] // 2
    p1, p3 = from_grp(p0, 1), from_grp(p0, 3)
    q1, q3 = from_tok(q0, dx=1), from_tok(q0, dx=3)
    p1, p3, q1, q3 = lax.optimization_barrier((p1, p3, q1, q3))
    p2a, p2b = from_grp(p1[:half], 1), from_grp(p3[half:], 3)
    q2a, q2b = from_tok(q1[:half], dx=1), from_tok(q3[half:], dx=3)
    normed_p, normed_q = input_norm(x[None], own, peer, norm_gain[None, :])

    marks_before = from_previous_chip(marks_chip)
    index = jnp.arange(rows, dtype=jnp.int32)
    index_chip = jnp.concatenate([index + core * rows, index + (1 - core) * rows])
    marks_k = jnp.concatenate([marks_before, marks_chip])[None, :]
    index_k = jnp.concatenate([jnp.full((2 * rows,), -1, jnp.int32), index_chip])[None, :]
    marks_q, index_q = marks_chip[:, None], index_chip[:, None]
    earlier = (marks_q == marks_k) & (index_k < index_q)
    offset = jnp.sum(earlier.astype(jnp.int32), axis=1)
    token_positions = (prefix_len + offset).astype(jnp.float32)
    half_width = head_dim // 2
    freqs = theta_base ** (-jnp.arange(half_width, dtype=jnp.float32) / half_width)
    angles = token_positions[:, None] * freqs[None, :]
    cosine, sine = jnp.cos(angles), jnp.sin(angles)
    cosine = jnp.concatenate([cosine, cosine], axis=1)
    sine = jnp.concatenate([-sine, sine], axis=1)

    qkv = joint_projection(
        y[None],
        normed_p,
        normed_q,
        [p0, p1, p2a, p2b, p3],
        [q0, q1, q2a, q2b, q3],
        cosine,
        sine,
        query_gain[None, :],
        key_norm_gain[None, :],
    )
    halo = from_previous_chip(qkv[2:])
    kv_got = from_tok(qkv[2:, rows:], dc=1)

    p2 = jnp.concatenate([p2a, p2b])
    q2 = jnp.concatenate([q2a, q2b])
    p_out = jnp.stack([p0, p1, p2, p3]).reshape(NY, NX, 384, 256)[:, :, 256:]
    q_out = jnp.stack([q0, q1, q2, q3]).reshape(NX, NY, 384, 256)[:, :, 256:]
    out_weights = jnp.concatenate([p_out, jnp.swapaxes(q_out, 0, 1)], axis=1)
    out_weights = out_weights.reshape(NY, 1024, 256)
    out_other = from_tok(out_weights, dc=1)

    suffix = suffix_attention(qkv, halo, marks_q, index_q, marks_k, index_k, scale)
    attended = prefix_attention(core[None], qkv, prefix, suffix, scale)
    attended_got = from_tok(attended[rows:], dc=1)
    projected = output_projection(
        jnp.stack([x, y, core]), attended[:rows], attended_got, out_weights, out_other
    )
    cache = in_core_order(core, qkv[2:, :rows], kv_got, 2)
    return (projected[None], cache[0][None], cache[1][None])


def solution(mesh):
    return jax.shard_map(
        per_device,
        mesh=mesh,
        in_specs=(
            P("grp", "tok", None),
            P("grp", "tok"),
            P("grp", "tok", None),
            P(),
            P(),
            P(),
            P(),
            P("tok", None),
            P("tok", None),
        ),
        out_specs=(P("grp", "tok", None), P("grp", "tok", None), P("grp", "tok", None)),
        check_vma=False,
    )
```

```python
import functools
import math

import jax
import jax.numpy as jnp
from jax import lax
from jax.experimental import pallas as pl
from jax.experimental.pallas import tpu as pltpu
from jax.sharding import PartitionSpec as P

NX, NZ, NC, NY = 4, 8, 2, 4

epsilon = 1e-06
theta_base = 1000000.0
floor_score = -1e30
VMEM_LIMIT = 56 * 1024 * 1024


def place(x, z, c):
    return (x * NZ + z) * NC + c


def from_tok(block, dx=0, dz=0, dc=0):
    route = [
        (place((x + dx) % NX, (z + dz) % NZ, (c + dc) % NC), place(x, z, c))
        for x in range(NX)
        for z in range(NZ)
        for c in range(NC)
    ]
    return lax.ppermute(block, "tok", route)


def from_grp(block, dy):
    return lax.ppermute(block, "grp", [((y + dy) % NY, y) for y in range(NY)])


def from_previous_chip(block):
    chips = NX * NZ
    route = [(p * NC + c, (p + 1) * NC + c) for p in range(chips - 1) for c in range(NC)]
    return lax.ppermute(block, "tok", route)


def in_core_order(core, mine, other, axis):
    first = jnp.where(core == 0, mine, other)
    second = jnp.where(core == 0, other, mine)
    return jnp.concatenate([first, second], axis=axis)


def norm_kernel(x_ref, own_ref, peer_ref, gain_ref, np_ref, nq_ref, scratch):
    half = own_ref.shape[0]
    gain = gain_ref[...].astype(jnp.float32)
    x = x_ref[0]
    for part, ref in enumerate((own_ref, peer_ref)):
        tokens = ref[...].astype(jnp.float32)
        mean = jnp.mean(tokens * tokens, axis=-1, keepdims=True)
        scratch[...] = (tokens * lax.rsqrt(mean + epsilon) * gain).astype(jnp.bfloat16)
        for j in range(NX):
            at = pl.multiple_of(((x + j) % NX) * 512, 512)
            np_ref[pl.ds(part * half, half), j * 256 : (j + 1) * 256] = scratch[:, pl.ds(at, 256)]
            at = pl.multiple_of(((x + j) % NX) * 512 + 256, 256)
            nq_ref[pl.ds(part * half, half), j * 256 : (j + 1) * 256] = scratch[:, pl.ds(at, 256)]


def input_norm(x, own, peer, gain):
    rows, width = own.shape
    out = jax.ShapeDtypeStruct((2 * rows, width // 2), jnp.bfloat16)
    vmem = pl.BlockSpec(memory_space=pltpu.VMEM)
    return pl.pallas_call(
        norm_kernel,
        out_shape=(out, out),
        in_specs=[pl.BlockSpec(memory_space=pltpu.SMEM), vmem, vmem, vmem],
        out_specs=(vmem, vmem),
        scratch_shapes=[pltpu.VMEM((rows, width), jnp.bfloat16)],
        compiler_params=pltpu.CompilerParams(vmem_limit_bytes=VMEM_LIMIT),
        name="input_norm",
    )(x, own, peer, gain)


def qkv_kernel(
    y_ref, np_ref, nq_ref, p0, p1, p2, p3, q0, q1, q2, q3, cos_ref, sin_ref, qg_ref, kg_ref,
    q_out, kv_out, acc
):
    step = pl.program_id(0)
    block = (y_ref[0] + step) % NY

    def dot(a, b):
        return jnp.dot(a, b, preferred_element_type=jnp.float32)

    for k, p in enumerate((p0, p1, p2, p3)):

        @pl.when(step == k)
        def _(p=p, k=k):
            total = dot(np_ref[...], p[...])
            for j, q in enumerate((q0, q1, q2, q3)):
                total = total + dot(
                    nq_ref[:, j * 256 : (j + 1) * 256], q[k * 256 : (k + 1) * 256, :]
                )
            acc[...] = total

    def turned(gain_ref, out):
        gain = gain_ref[...].astype(jnp.float32)
        for h in range(2):
            a = acc[:, h * 128 : (h + 1) * 128]
            mean = jnp.mean(a * a, axis=-1, keepdims=True)
            a = a * lax.rsqrt(mean + epsilon) * gain
            a = a * cos_ref[...] + pltpu.roll(a, 64, 1) * sin_ref[...]
            out[0, :, h * 128 : (h + 1) * 128] = a.astype(jnp.bfloat16)

    @pl.when(block < 2)
    def _():
        turned(qg_ref, q_out)

    @pl.when(block == 2)
    def _():
        turned(kg_ref, kv_out)

    @pl.when(block == 3)
    def _():
        kv_out[0] = acc[...].astype(jnp.bfloat16)


def query_block(i, y_ref):
    block = (y_ref[0] + i) % NY
    return jnp.where(block < 2, block, jnp.where(i >= block - 1, 1, 0)), 0, 0


def key_value_block(i, y_ref):
    block = (y_ref[0] + i) % NY
    return jnp.where(block >= 2, block - 2, jnp.where(i >= block + 1, 1, 0)), 0, 0


def joint_projection(y, normed_p, normed_q, p, q, cosine, sine, query_gain, key_gain):
    rows = normed_p.shape[0]
    whole = lambda a: pl.BlockSpec(a.shape, lambda i, y_ref: (0,) * a.ndim)
    args = [normed_p, normed_q, *p, *q, cosine, sine, query_gain, key_gain]
    out = jax.ShapeDtypeStruct((2, rows, 256), jnp.bfloat16)
    return pl.pallas_call(
        qkv_kernel,
        out_shape=(out, out),
        grid_spec=pltpu.PrefetchScalarGridSpec(
            num_scalar_prefetch=1,
            grid=(NY,),
            in_specs=[whole(a) for a in args],
            out_specs=(
                pl.BlockSpec((1, rows, 256), query_block),
                pl.BlockSpec((1, rows, 256), key_value_block),
            ),
            scratch_shapes=[pltpu.VMEM((rows, 256), jnp.float32)],
        ),
        compiler_params=pltpu.CompilerParams(
            dimension_semantics=("arbitrary",), vmem_limit_bytes=VMEM_LIMIT
        ),
        cost_estimate=pl.CostEstimate(
            flops=2 * rows * 2048 * 1024, transcendentals=0, bytes_accessed=8 << 20
        ),
        name="joint_projection",
    )(y, *args)


LANES = (((1,), (1,)), ((), ()))


def fold(op, blocks):
    return functools.reduce(
        op, [b[:, i : i + 128] for b in blocks for i in range(0, b.shape[1], 128)]
    )


def row_max(blocks):
    return jnp.max(fold(jnp.maximum, blocks), axis=-1, keepdims=True)


def prefix_kernel(scale, core_ref, q_ref, k_ref, v_ref, acc_ref, top_ref, total_ref):
    rows = q_ref.shape[1]
    step = 512
    starts = range(0, k_ref.shape[0], step)
    q = jnp.concatenate([q_ref[0, :, :128], q_ref[0, :, 128:]], axis=0)
    scores = [
        lax.dot_general(q, k_ref[i : i + step, :], LANES, preferred_element_type=jnp.float32)
        for i in starts
    ]
    top = row_max(scores)
    total = jnp.zeros(q.shape, jnp.float32)
    acc = jnp.zeros(q.shape, jnp.float32)
    for s, i in zip(scores, starts):
        w = jnp.exp2((s - top) * scale)
        total = total + fold(jnp.add, [w])
        acc = acc + jnp.dot(
            w.astype(jnp.bfloat16), v_ref[i : i + step, :], preferred_element_type=jnp.float32
        )
    total = jnp.sum(total, axis=-1, keepdims=True)
    for h in range(2):
        at = slice(h * rows, (h + 1) * rows)
        acc_ref[h], top_ref[h], total_ref[h] = acc[at], top[at], total[at]


def prefix_attention(core, qkv, prefix, scale):
    rows = qkv.shape[1]
    keys = prefix.shape[0]
    stat = jax.ShapeDtypeStruct((4, rows, 1), jnp.float32)
    pair = lambda width: pl.BlockSpec((2, rows, width), lambda g, c: (g, 0, 0))
    return pl.pallas_call(
        functools.partial(prefix_kernel, scale),
        out_shape=(jax.ShapeDtypeStruct((4, rows, 128), jnp.float32), stat, stat),
        grid_spec=pltpu.PrefetchScalarGridSpec(
            num_scalar_prefetch=1,
            grid=(2,),
            in_specs=[
                pl.BlockSpec((1, rows, 256), lambda g, c: (g, 0, 0)),
                pl.BlockSpec((keys, 128), lambda g, c: (0, 2 * c[0] + g)),
                pl.BlockSpec((keys, 128), lambda g, c: (0, 4 + 2 * c[0] + g)),
            ],
            out_specs=(pair(128), pair(1), pair(1)),
        ),
        compiler_params=pltpu.CompilerParams(
            dimension_semantics=("arbitrary",), vmem_limit_bytes=VMEM_LIMIT
        ),
        cost_estimate=pl.CostEstimate(
            flops=4 * 4 * rows * keys * 128, transcendentals=4 * rows * keys, bytes_accessed=4 << 20
        ),
        name="prefix_attention",
    )(core, qkv, prefix, prefix)


def suffix_kernel(
    scale, q_ref, ko_ref, vo_ref, kh_ref, vh_ref, acc_ref, top_ref, total_ref,
    bias, own_ref, peer_ref
):
    rows, chip = q_ref.shape[1], ko_ref.shape[1]

    for h in range(2):
        at = slice(h * 128, (h + 1) * 128)
        q = q_ref[0, :, at]
        scores = [
            lax.dot_general(q, k[0], LANES, preferred_element_type=jnp.float32)
            + bias[:, i * chip : (i + 1) * chip]
            for i, k in enumerate((kh_ref, ko_ref))
        ]
        before = top_ref[h]
        top = jnp.maximum(before, row_max(scores))
        shrink = jnp.exp2((before - top) * scale)
        total = jnp.zeros((rows, 128), jnp.float32)
        acc = acc_ref[h] * shrink
        for s, v in zip(scores, (vh_ref, vo_ref)):
            w = jnp.exp2((s - top) * scale)
            total = total + fold(jnp.add, [w])
            acc = acc + jnp.dot(w.astype(jnp.bfloat16), v[0], preferred_element_type=jnp.float32)
        total = total_ref[h] * shrink + jnp.sum(total, axis=-1, keepdims=True)
        out = (acc / total).astype(jnp.bfloat16)
        own_ref[:, at] = out[: rows // 2]
        peer_ref[:, at] = out[rows // 2 :]


def suffix_attention(queries, own, halo, partial, bias, scale):
    rows = queries.shape[1]
    pair = lambda width: pl.BlockSpec((2, rows, width), lambda g: (g, 0, 0))
    head = lambda block: pl.BlockSpec((1, rows, 128), lambda g: (block, 0, g))
    out = jax.ShapeDtypeStruct((rows // 2, 512), jnp.bfloat16)
    out_spec = pl.BlockSpec((rows // 2, 256), lambda g: (0, g))
    return pl.pallas_call(
        functools.partial(suffix_kernel, scale),
        out_shape=(out, out),
        grid=(2,),
        in_specs=[
            pl.BlockSpec((1, rows, 256), lambda g: (g, 0, 0)),
            head(0),
            head(1),
            head(0),
            head(1),
            pair(128),
            pair(1),
            pair(1),
            pl.BlockSpec(bias.shape, lambda g: (0, 0)),
        ],
        out_specs=(out_spec, out_spec),
        compiler_params=pltpu.CompilerParams(
            dimension_semantics=("arbitrary",), vmem_limit_bytes=VMEM_LIMIT
        ),
        cost_estimate=pl.CostEstimate(
            flops=4 * 4 * rows * 1024 * 128, transcendentals=4 * rows * 1024, bytes_accessed=4 << 20
        ),
        name="suffix_attention",
    )(queries, own, own, halo, halo, *partial, bias)


def out_kernel(place_ref, mine_ref, other_ref, *refs):
    *weights, out_ref, heads = refs
    x, core = place_ref[0], place_ref[1]
    heads[:, pl.ds(pl.multiple_of(core * 512, 512), 512)] = mine_ref[...]
    heads[:, pl.ds(pl.multiple_of((1 - core) * 512, 512), 512)] = other_ref[...]
    for c, strips in ((core, weights[:NX]), (1 - core, weights[NX:])):
        total = jnp.zeros((mine_ref.shape[0], 1024), jnp.float32)
        for j, strip in enumerate(strips):
            at = pl.multiple_of(((x + j) % NX) * 256, 256)
            total = total + jnp.dot(
                heads[:, pl.ds(at, 256)], strip[...], preferred_element_type=jnp.float32
            )
        out_ref[:, pl.ds(pl.multiple_of(c * 1024, 1024), 1024)] = total.astype(jnp.bfloat16)


def output_projection(x, core, mine, other, strips, strips_other):
    rows = mine.shape[0]
    vmem = pl.BlockSpec(memory_space=pltpu.VMEM)
    args = [mine, other, *strips, *strips_other]
    return pl.pallas_call(
        out_kernel,
        out_shape=jax.ShapeDtypeStruct((rows, 2048), jnp.bfloat16),
        in_specs=[pl.BlockSpec(memory_space=pltpu.SMEM)] + [vmem] * len(args),
        out_specs=vmem,
        scratch_shapes=[pltpu.VMEM((rows, 1024), jnp.bfloat16)],
        compiler_params=pltpu.CompilerParams(vmem_limit_bytes=VMEM_LIMIT),
        cost_estimate=pl.CostEstimate(
            flops=2 * rows * 1024 * 2048, transcendentals=0, bytes_accessed=6 << 20
        ),
        name="output_projection",
    )(jnp.stack([x, core]), *args)


def pack_kernel(p0, p1, p2, p3, q0, q1, q2, q3, p_ref, q_ref, prefix_ref):
    for k, (p, q) in enumerate(((p0, q0), (p1, q1), (p2, q2), (p3, q3))):
        p_ref[k * 256 : (k + 1) * 256, :] = p[:256, :]
        q_ref[k * 256 : (k + 1) * 256, :] = q[...]
        for i in range(4):
            prefix_ref[k * 32 : (k + 1) * 32, i * 256 : (i + 1) * 256] = p[
                256 + 32 * i : 288 + 32 * i, :
            ]


def pack(p_all, q_all):
    vmem = pl.BlockSpec(memory_space=pltpu.VMEM)
    strip = jax.ShapeDtypeStruct((1024, 256), jnp.bfloat16)
    return pl.pallas_call(
        pack_kernel,
        out_shape=(strip, strip, jax.ShapeDtypeStruct((128, 1024), jnp.bfloat16)),
        in_specs=[vmem] * 8,
        out_specs=(vmem, vmem, vmem),
        compiler_params=pltpu.CompilerParams(vmem_limit_bytes=VMEM_LIMIT),
        name="pack",
    )(*p_all, *q_all)


GROUP_ZC = [[place(x, z, c) for z in range(NZ) for c in range(NC)] for x in range(NX)]


def per_device(
    hidden_in, doc_ids, prefix_kv, prefix_owner, norm_gain, query_gain, key_norm_gain, w_qkv, w_out
):
    rows = hidden_in.shape[1]
    head_dim = query_gain.shape[0]
    prefix_len = prefix_kv.shape[1] * lax.axis_size("tok")
    scale = head_dim ** (-0.5) * math.log2(math.e)
    place_tok = lax.axis_index("tok")
    y = lax.axis_index("grp")
    x, z, core = place_tok // (NZ * NC), (place_tok // NC) % NZ, place_tok % NC

    own = hidden_in[0]
    out_strip = lax.all_gather(w_out, "tok", axis_index_groups=GROUP_ZC, tiled=True)
    owners = [prefix_kv[0]] + [from_grp(prefix_kv[0], d) for d in range(1, NY)]
    owner = (prefix_owner[y] - y) % NY

    def columns(c):
        start = jnp.where(y < 2, 512 * c + 256 * y, 512 * y + 256 * c)
        return lax.dynamic_slice(w_qkv, (jnp.int32(0), start), (w_qkv.shape[0], 256))

    marks = (doc_ids + 1).astype(jnp.bfloat16)
    first = jnp.concatenate(
        [
            jnp.concatenate([columns(0), columns(1)], axis=1),
            jnp.pad(marks, ((0, 7), (0, 256))),
        ],
        axis=0,
    )
    both = lax.all_gather(first, "tok", axis_index_groups=GROUP_ZC)
    peer = from_tok(own, dc=1)
    both, owners, peer, norm_gain, query_gain, key_norm_gain = lax.optimization_barrier(
        (both, owners, peer, norm_gain, query_gain, key_norm_gain)
    )

    marks_x = both[:, 32, :256]
    strip = lax.dynamic_slice_in_dim(both[:, :32], core * 256, 256, 2).reshape(512, 256)
    prefix_rows = lax.dynamic_index_in_dim(jnp.stack(owners), owner, 0, keepdims=False)
    p_own = jnp.concatenate(
        [strip[:256]]
        + [prefix_rows[:, i * 256 : (i + 1) * 256] for i in range(4)]
        + [jnp.pad(marks_x[14:], ((0, 6), (0, 0)))]
    )
    q_own = strip[256:]
    p_all = [p_own] + [from_tok(p_own, dx=d) for d in (2, 1, 3)]
    p_all = [p_all[0], p_all[2], p_all[1], p_all[3]]
    q_all = [q_own] + [from_grp(q_own, d) for d in range(1, NY)]
    p_all, q_all = lax.optimization_barrier((p_all, q_all))

    p0, q0, prefix_part = pack(p_all, q_all)
    p2 = from_grp(p0, 2)
    p1, p3 = from_grp(p0, 1), from_grp(p0, 3)
    q1, q3 = from_tok(q0, dx=1), from_tok(q0, dx=3)
    q2 = from_tok(q0, dx=2)
    prefix = lax.all_gather(prefix_part, "tok", axis_index_groups=GROUP_ZC, tiled=True)

    normed_p, normed_q = input_norm(x[None], own, peer, norm_gain[None, :])
    marks_left = jnp.where(x > 0, p_all[3][384:386], 0)
    near = lax.dynamic_slice_in_dim(
        jnp.concatenate([marks_left, marks_x]).astype(jnp.float32), 2 * z, 4, 0
    )
    near = near.reshape(2, 2, rows)
    near = jnp.where(core == 0, near, near[:, ::-1])
    marks_k = near.reshape(1, 4 * rows)
    marks_q = near[1].reshape(2 * rows, 1)
    index = jnp.arange(rows, dtype=jnp.int32)
    index_chip = jnp.concatenate([index + core * rows, index + (1 - core) * rows])
    index_k = jnp.concatenate([jnp.full((2 * rows,), -1, jnp.int32), index_chip])[None, :]
    index_q = index_chip[:, None]
    earlier = (marks_q == marks_k) & (index_k < index_q)
    allowed = (marks_q == marks_k) & (index_k <= index_q)
    bias = jnp.where(allowed, jnp.float32(0), jnp.float32(floor_score))
    offset = jnp.sum(earlier.astype(jnp.int32), axis=1)
    token_positions = (prefix_len + offset).astype(jnp.float32)
    half_width = head_dim // 2
    freqs = theta_base ** (-jnp.arange(half_width, dtype=jnp.float32) / half_width)
    angles = token_positions[:, None] * freqs[None, :]
    cosine, sine = jnp.cos(angles), jnp.sin(angles)
    cosine = jnp.concatenate([cosine, cosine], axis=1)
    sine = jnp.concatenate([-sine, sine], axis=1)
    gains = (query_gain[None, :], key_norm_gain[None, :])

    under = (normed_p, normed_q, cosine, sine, bias, gains)
    pieces = ([p0, p1, p2, p3], [q0, q1, q2, q3])

    out_mine = lax.dynamic_slice_in_dim(out_strip, core * 1024, 1024, 1)
    out_mine, pieces, under = lax.optimization_barrier((out_mine, pieces, under))
    normed_p, normed_q, cosine, sine, bias, gains = under
    strips = [out_mine] + [from_tok(out_mine, dx=d) for d in range(1, NX)]
    queries, kv = joint_projection(y[None], normed_p, normed_q, *pieces, cosine, sine, *gains)
    halo = from_previous_chip(kv)

    partial = prefix_attention(core[None], queries, prefix, scale)
    strips, partial, kv_sent = lax.optimization_barrier((strips, partial, kv))
    strips_other = [from_tok(s, dc=1) for s in strips]
    kv_got = from_tok(kv_sent, dc=1)[:, rows:]
    mine, others = suffix_attention(queries, kv, halo, partial, bias, scale)
    got = from_tok(others, dc=1)
    projected = output_projection(x, core, mine, got, strips, strips_other)
    cache = in_core_order(core, kv[:, :rows], kv_got, 2)
    return (projected[None], cache[0][None], cache[1][None])


def solution(mesh):
    return jax.shard_map(
        per_device,
        mesh=mesh,
        in_specs=(
            P("grp", "tok", None),
            P("grp", "tok"),
            P("grp", "tok", None),
            P(),
            P(),
            P(),
            P(),
            P("tok", None),
            P("tok", None),
        ),
        out_specs=(P("grp", "tok", None), P("grp", "tok", None), P("grp", "tok", None)),
        check_vma=False,
    )
```

```python
import functools
import math

import jax
import jax.numpy as jnp
from jax import lax
from jax.experimental import pallas as pl
from jax.experimental.pallas import tpu as pltpu
from jax.sharding import PartitionSpec as P

NX, NZ, NC, NY = 4, 8, 2, 4

epsilon = 1e-06
theta_base = 1000000.0
floor_score = -1e30
VMEM_LIMIT = 56 * 1024 * 1024


def place(x, z, c):
    return (x * NZ + z) * NC + c


def from_tok(block, dx=0, dz=0, dc=0):
    route = [
        (place((x + dx) % NX, (z + dz) % NZ, (c + dc) % NC), place(x, z, c))
        for x in range(NX)
        for z in range(NZ)
        for c in range(NC)
    ]
    return lax.ppermute(block, "tok", route)


def from_grp(block, dy):
    return lax.ppermute(block, "grp", [((y + dy) % NY, y) for y in range(NY)])


def from_previous_chip(block):
    chips = NX * NZ
    route = [(p * NC + c, (p + 1) * NC + c) for p in range(chips - 1) for c in range(NC)]
    return lax.ppermute(block, "tok", route)


def in_core_order(core, mine, other, axis):
    first = jnp.where(core == 0, mine, other)
    second = jnp.where(core == 0, other, mine)
    return jnp.concatenate([first, second], axis=axis)


def norm_kernel(x_ref, own_ref, peer_ref, gain_ref, np_ref, nq_ref, scratch):
    half = own_ref.shape[0]
    gain = gain_ref[...].astype(jnp.float32)
    x = x_ref[0]
    for part, ref in enumerate((own_ref, peer_ref)):
        tokens = ref[...].astype(jnp.float32)
        mean = jnp.mean(tokens * tokens, axis=-1, keepdims=True)
        scratch[...] = (tokens * lax.rsqrt(mean + epsilon) * gain).astype(jnp.bfloat16)
        for j in range(NX):
            at = pl.multiple_of(((x + j) % NX) * 512, 512)
            np_ref[pl.ds(part * half, half), j * 256 : (j + 1) * 256] = scratch[:, pl.ds(at, 256)]
            at = pl.multiple_of(((x + j) % NX) * 512 + 256, 256)
            nq_ref[pl.ds(part * half, half), j * 256 : (j + 1) * 256] = scratch[:, pl.ds(at, 256)]


def input_norm(x, own, peer, gain):
    rows, width = own.shape
    out = jax.ShapeDtypeStruct((2 * rows, width // 2), jnp.bfloat16)
    vmem = pl.BlockSpec(memory_space=pltpu.VMEM)
    return pl.pallas_call(
        norm_kernel,
        out_shape=(out, out),
        in_specs=[pl.BlockSpec(memory_space=pltpu.SMEM), vmem, vmem, vmem],
        out_specs=(vmem, vmem),
        scratch_shapes=[pltpu.VMEM((rows, width), jnp.bfloat16)],
        compiler_params=pltpu.CompilerParams(vmem_limit_bytes=VMEM_LIMIT),
        name="input_norm",
    )(x, own, peer, gain)


def qkv_kernel(
    y_ref, np_ref, nq_ref, p0, p1, p2, p3, q0, q1, q2, q3, cos_ref, sin_ref, qg_ref, kg_ref,
    q_out, kv_out, acc
):
    step = pl.program_id(0)
    block = (y_ref[0] + step) % NY

    def dot(a, b):
        return jnp.dot(a, b, preferred_element_type=jnp.float32)

    for k, p in enumerate((p0, p1, p2, p3)):

        @pl.when(step == k)
        def _(p=p, k=k):
            total = dot(np_ref[...], p[...])
            for j, q in enumerate((q0, q1, q2, q3)):
                total = total + dot(
                    nq_ref[:, j * 256 : (j + 1) * 256], q[k * 256 : (k + 1) * 256, :]
                )
            acc[...] = total

    def turned(gain_ref, out):
        gain = gain_ref[...].astype(jnp.float32)
        for h in range(2):
            a = acc[:, h * 128 : (h + 1) * 128]
            mean = jnp.mean(a * a, axis=-1, keepdims=True)
            a = a * lax.rsqrt(mean + epsilon) * gain
            a = a * cos_ref[...] + pltpu.roll(a, 64, 1) * sin_ref[...]
            out[0, :, h * 128 : (h + 1) * 128] = a.astype(jnp.bfloat16)

    @pl.when(block < 2)
    def _():
        turned(qg_ref, q_out)

    @pl.when(block == 2)
    def _():
        turned(kg_ref, kv_out)

    @pl.when(block == 3)
    def _():
        kv_out[0] = acc[...].astype(jnp.bfloat16)


def query_block(i, y_ref):
    block = (y_ref[0] + i) % NY
    return jnp.where(block < 2, block, jnp.where(i >= block - 1, 1, 0)), 0, 0


def key_value_block(i, y_ref):
    block = (y_ref[0] + i) % NY
    return jnp.where(block >= 2, block - 2, jnp.where(i >= block + 1, 1, 0)), 0, 0


def joint_projection(y, normed_p, normed_q, p, q, cosine, sine, query_gain, key_gain):
    rows = normed_p.shape[0]
    whole = lambda a: pl.BlockSpec(a.shape, lambda i, y_ref: (0,) * a.ndim)
    args = [normed_p, normed_q, *p, *q, cosine, sine, query_gain, key_gain]
    out = jax.ShapeDtypeStruct((2, rows, 256), jnp.bfloat16)
    return pl.pallas_call(
        qkv_kernel,
        out_shape=(out, out),
        grid_spec=pltpu.PrefetchScalarGridSpec(
            num_scalar_prefetch=1,
            grid=(NY,),
            in_specs=[whole(a) for a in args],
            out_specs=(
                pl.BlockSpec((1, rows, 256), query_block),
                pl.BlockSpec((1, rows, 256), key_value_block),
            ),
            scratch_shapes=[pltpu.VMEM((rows, 256), jnp.float32)],
        ),
        compiler_params=pltpu.CompilerParams(
            dimension_semantics=("arbitrary",), vmem_limit_bytes=VMEM_LIMIT
        ),
        cost_estimate=pl.CostEstimate(
            flops=2 * rows * 2048 * 1024, transcendentals=0, bytes_accessed=8 << 20
        ),
        name="joint_projection",
    )(y, *args)


LANES = (((1,), (1,)), ((), ()))


def fold(op, blocks):
    return functools.reduce(
        op, [b[:, i : i + 128] for b in blocks for i in range(0, b.shape[1], 128)]
    )


def row_max(blocks):
    return jnp.max(fold(jnp.maximum, blocks), axis=-1, keepdims=True)


def prefix_kernel(scale, core_ref, q_ref, k_ref, v_ref, acc_ref, stat_ref):
    rows, step = 256, 512
    starts = range(0, k_ref.shape[0], step)
    for r in range(0, q_ref.shape[1], rows):
        for h in range(2):
            q = q_ref[0, r : r + rows, h * 128 : (h + 1) * 128]
            scores = [
                lax.dot_general(
                    q, k_ref[i : i + step, :], LANES, preferred_element_type=jnp.float32
                )
                for i in starts
            ]
            top = row_max(scores)
            total = jnp.zeros(q.shape, jnp.float32)
            acc = jnp.zeros(q.shape, jnp.float32)
            for s, i in zip(scores, starts):
                w = jnp.exp2((s - top) * scale)
                total = total + fold(jnp.add, [w])
                acc = acc + jnp.dot(
                    w.astype(jnp.bfloat16),
                    v_ref[i : i + step, :],
                    preferred_element_type=jnp.float32,
                )
            acc_ref[h, r : r + rows, :] = acc
            stat_ref[h, r : r + rows, 0:1] = top
            stat_ref[h, r : r + rows, 1:2] = jnp.sum(total, axis=-1, keepdims=True)


def prefix_attention(core, qkv, prefix, scale):
    rows = qkv.shape[1]
    keys = prefix.shape[0]
    out = jax.ShapeDtypeStruct((4, rows, 128), jnp.float32)
    pair = pl.BlockSpec((2, rows, 128), lambda g, c: (g, 0, 0))
    return pl.pallas_call(
        functools.partial(prefix_kernel, scale),
        out_shape=(out, out),
        grid_spec=pltpu.PrefetchScalarGridSpec(
            num_scalar_prefetch=1,
            grid=(2,),
            in_specs=[
                pl.BlockSpec((1, rows, 256), lambda g, c: (g, 0, 0)),
                pl.BlockSpec((keys, 128), lambda g, c: (0, 2 * c[0] + g)),
                pl.BlockSpec((keys, 128), lambda g, c: (0, 4 + 2 * c[0] + g)),
            ],
            out_specs=(pair, pair),
        ),
        compiler_params=pltpu.CompilerParams(
            dimension_semantics=("arbitrary",), vmem_limit_bytes=VMEM_LIMIT
        ),
        cost_estimate=pl.CostEstimate(
            flops=4 * 4 * rows * keys * 128, transcendentals=4 * rows * keys, bytes_accessed=4 << 20
        ),
        name="prefix_attention",
    )(core, qkv, prefix, prefix)


def suffix_kernel(
    scale, core_ref, q_ref, ko_ref, vo_ref, kh_ref, vh_ref, acc_ref, stat_ref, bias_ref,
    own_ref, peer_ref
):
    core = core_ref[0]
    rows = own_ref.shape[0]
    zero = pl.ds(pl.multiple_of(core * rows, rows), rows)
    one = pl.ds(pl.multiple_of((1 - core) * rows, rows), rows)
    for r, out_ref in enumerate((own_ref, peer_ref)):
        block = slice(r * rows, (r + 1) * rows)
        third = [jnp.where(core == r, h[0, block, :], o[0, block, :])
                 for h, o in ((kh_ref, ko_ref), (vh_ref, vo_ref))]
        keys = [kh_ref[0, one, :], ko_ref[0, zero, :], third[0]]
        values = [vh_ref[0, one, :], vo_ref[0, zero, :], third[1]]
        for h in range(2):
            q = q_ref[0, block, h * 128 : (h + 1) * 128]
            scores = [
                lax.dot_general(q, k, LANES, preferred_element_type=jnp.float32)
                + bias_ref[r, :, i * rows : (i + 1) * rows].astype(jnp.float32)
                for i, k in enumerate(keys)
            ]
            before = stat_ref[h, block, 0:1]
            top = jnp.maximum(before, row_max(scores))
            shrink = jnp.exp2((before - top) * scale)
            weights = [jnp.exp2((s - top) * scale) for s in scores]
            total = jnp.sum(fold(jnp.add, weights), axis=-1, keepdims=True)
            total = stat_ref[h, block, 1:2] * shrink + total
            acc = acc_ref[h, block, :] * shrink
            for w, v in zip(weights, values):
                acc = acc + jnp.dot(w.astype(jnp.bfloat16), v, preferred_element_type=jnp.float32)
            out_ref[:, h * 128 : (h + 1) * 128] = (acc / total).astype(jnp.bfloat16)


def suffix_attention(core, queries, own, halo, partial, bias, scale):
    rows = queries.shape[1]
    pair = pl.BlockSpec((2, rows, 128), lambda g, c: (g, 0, 0))
    head = lambda block: pl.BlockSpec((1, rows, 128), lambda g, c: (block, 0, g))
    out = jax.ShapeDtypeStruct((rows // 2, 512), jnp.bfloat16)
    out_spec = pl.BlockSpec((rows // 2, 256), lambda g, c: (0, g))
    return pl.pallas_call(
        functools.partial(suffix_kernel, scale),
        out_shape=(out, out),
        grid_spec=pltpu.PrefetchScalarGridSpec(
            num_scalar_prefetch=1,
            grid=(2,),
            in_specs=[
                pl.BlockSpec((1, rows, 256), lambda g, c: (g, 0, 0)),
                head(0),
                head(1),
                head(0),
                head(1),
                pair,
                pair,
                pl.BlockSpec(bias.shape, lambda g, c: (0, 0, 0)),
            ],
            out_specs=(out_spec, out_spec),
        ),
        compiler_params=pltpu.CompilerParams(
            dimension_semantics=("arbitrary",), vmem_limit_bytes=VMEM_LIMIT
        ),
        cost_estimate=pl.CostEstimate(
            flops=4 * 4 * rows * 768 * 128, transcendentals=4 * rows * 768, bytes_accessed=4 << 20
        ),
        name="suffix_attention",
    )(core, queries, own, own, halo, halo, *partial, bias)


def out_kernel(place_ref, mine_ref, other_ref, *refs):
    *weights, out_ref, heads = refs
    x, core = place_ref[0], place_ref[1]
    heads[:, pl.ds(pl.multiple_of(core * 512, 512), 512)] = mine_ref[...]
    heads[:, pl.ds(pl.multiple_of((1 - core) * 512, 512), 512)] = other_ref[...]
    for c, strips in ((core, weights[:NX]), (1 - core, weights[NX:])):
        total = jnp.zeros((mine_ref.shape[0], 1024), jnp.float32)
        for j, strip in enumerate(strips):
            at = pl.multiple_of(((x + j) % NX) * 256, 256)
            total = total + jnp.dot(
                heads[:, pl.ds(at, 256)], strip[...], preferred_element_type=jnp.float32
            )
        out_ref[:, pl.ds(pl.multiple_of(c * 1024, 1024), 1024)] = total.astype(jnp.bfloat16)


def output_projection(x, core, mine, other, strips, strips_other):
    rows = mine.shape[0]
    vmem = pl.BlockSpec(memory_space=pltpu.VMEM)
    args = [mine, other, *strips, *strips_other]
    return pl.pallas_call(
        out_kernel,
        out_shape=jax.ShapeDtypeStruct((rows, 2048), jnp.bfloat16),
        in_specs=[pl.BlockSpec(memory_space=pltpu.SMEM)] + [vmem] * len(args),
        out_specs=vmem,
        scratch_shapes=[pltpu.VMEM((rows, 1024), jnp.bfloat16)],
        compiler_params=pltpu.CompilerParams(vmem_limit_bytes=VMEM_LIMIT),
        cost_estimate=pl.CostEstimate(
            flops=2 * rows * 1024 * 2048, transcendentals=0, bytes_accessed=6 << 20
        ),
        name="output_projection",
    )(jnp.stack([x, core]), *args)


def pack_kernel(p0, p1, p2, p3, q0, q1, q2, q3, p_ref, q_ref, prefix_ref):
    for k, (p, q) in enumerate(((p0, q0), (p1, q1), (p2, q2), (p3, q3))):
        p_ref[k * 256 : (k + 1) * 256, :] = p[:256, :]
        q_ref[k * 256 : (k + 1) * 256, :] = q[...]
        for i in range(4):
            prefix_ref[k * 32 : (k + 1) * 32, i * 256 : (i + 1) * 256] = p[
                256 + 32 * i : 288 + 32 * i, :
            ]


def pack(p_all, q_all):
    vmem = pl.BlockSpec(memory_space=pltpu.VMEM)
    strip = jax.ShapeDtypeStruct((1024, 256), jnp.bfloat16)
    return pl.pallas_call(
        pack_kernel,
        out_shape=(strip, strip, jax.ShapeDtypeStruct((128, 1024), jnp.bfloat16)),
        in_specs=[vmem] * 8,
        out_specs=(vmem, vmem, vmem),
        compiler_params=pltpu.CompilerParams(vmem_limit_bytes=VMEM_LIMIT),
        name="pack",
    )(*p_all, *q_all)


GROUP_ZC = [[place(x, z, c) for z in range(NZ) for c in range(NC)] for x in range(NX)]


def per_device(
    hidden_in, doc_ids, prefix_kv, prefix_owner, norm_gain, query_gain, key_norm_gain, w_qkv, w_out
):
    rows = hidden_in.shape[1]
    head_dim = query_gain.shape[0]
    prefix_len = prefix_kv.shape[1] * lax.axis_size("tok")
    scale = head_dim ** (-0.5) * math.log2(math.e)
    place_tok = lax.axis_index("tok")
    y = lax.axis_index("grp")
    x, z, core = place_tok // (NZ * NC), (place_tok // NC) % NZ, place_tok % NC

    own = hidden_in[0]
    out_strip = lax.all_gather(w_out, "tok", axis_index_groups=GROUP_ZC, tiled=True)
    owners = [prefix_kv[0]] + [from_grp(prefix_kv[0], d) for d in range(1, NY)]
    owner = (prefix_owner[y] - y) % NY

    def columns(c):
        start = jnp.where(y < 2, 512 * c + 256 * y, 512 * y + 256 * c)
        return lax.dynamic_slice(w_qkv, (jnp.int32(0), start), (w_qkv.shape[0], 256))

    marks = (doc_ids + 1).astype(jnp.bfloat16)
    first = jnp.concatenate(
        [
            jnp.concatenate([columns(0), columns(1)], axis=1),
            jnp.pad(marks, ((0, 7), (0, 256))),
        ],
        axis=0,
    )
    both = lax.all_gather(first, "tok", axis_index_groups=GROUP_ZC)
    peer = from_tok(own, dc=1)
    both, owners, peer, query_gain, key_norm_gain = lax.optimization_barrier(
        (both, owners, peer, query_gain, key_norm_gain)
    )

    marks_x = both[:, 32, :256]
    strip = lax.dynamic_slice_in_dim(both[:, :32], core * 256, 256, 2).reshape(512, 256)
    prefix_rows = lax.dynamic_index_in_dim(jnp.stack(owners), owner, 0, keepdims=False)
    p_own = jnp.concatenate(
        [strip[:256]]
        + [prefix_rows[:, i * 256 : (i + 1) * 256] for i in range(4)]
        + [jnp.pad(marks_x[14:], ((0, 6), (0, 0)))]
    )
    q_own = strip[256:]
    p_all = [p_own] + [from_tok(p_own, dx=d) for d in (2, 1, 3)]
    p_all = [p_all[0], p_all[2], p_all[1], p_all[3]]
    q_all = [q_own] + [from_grp(q_own, d) for d in range(1, NY)]
    p_all, q_all = lax.optimization_barrier((p_all, q_all))

    p0, q0, prefix_part = pack(p_all, q_all)
    p2 = from_grp(p0, 2)
    p1, p3 = from_grp(p0, 1), from_grp(p0, 3)
    q1, q3 = from_tok(q0, dx=1), from_tok(q0, dx=3)
    q2 = from_tok(q0, dx=2)
    prefix = lax.all_gather(prefix_part, "tok", axis_index_groups=GROUP_ZC, tiled=True)

    own, peer, norm_gain, p1 = lax.optimization_barrier((own, peer, norm_gain, p1))
    normed_p, normed_q = input_norm(x[None], own, peer, norm_gain[None, :])
    marks_left = jnp.where(x > 0, p_all[3][384:386], 0)
    near = lax.dynamic_slice_in_dim(
        jnp.concatenate([marks_left, marks_x]).astype(jnp.float32), 2 * z, 4, 0
    )
    row = lax.broadcasted_iota(jnp.int32, (rows, rows), 0)
    column = lax.broadcasted_iota(jnp.int32, (rows, rows), 1)
    bias, offset = [], []
    for part in range(2):
        upper = (core + part) % 2
        marks_q = lax.dynamic_index_in_dim(near, 2 + upper, 0, keepdims=False)[:, None]
        third = jnp.where(upper == 0, near[0], near[3])
        counted = 0
        for keys, whole in ((near[1], True), (near[2], upper == 1), (third, upper == 0)):
            same = marks_q == keys[None, :]
            seen = same & ((column <= row) | whole)
            bias.append(jnp.where(seen, 0.0, floor_score).astype(jnp.bfloat16))
            counted += jnp.sum((same & ((column < row) | whole)).astype(jnp.int32), axis=1)
        offset.append(counted)
    bias = jnp.stack(
        [jnp.concatenate(bias[:3], axis=1), jnp.concatenate(bias[3:], axis=1)]
    )
    offset = jnp.concatenate(offset)
    token_positions = (prefix_len + offset).astype(jnp.float32)
    half_width = head_dim // 2
    freqs = theta_base ** (-jnp.arange(half_width, dtype=jnp.float32) / half_width)
    angles = token_positions[:, None] * freqs[None, :]
    cosine, sine = jnp.cos(angles), jnp.sin(angles)
    cosine = jnp.concatenate([cosine, cosine], axis=1)
    sine = jnp.concatenate([-sine, sine], axis=1)
    gains = (query_gain[None, :], key_norm_gain[None, :])

    under = (normed_p, normed_q, cosine, sine, bias, gains)
    pieces = ([p0, p1, p2, p3], [q0, q1, q2, q3])

    out_mine = lax.dynamic_slice_in_dim(out_strip, core * 1024, 1024, 1)
    out_mine, pieces, under = lax.optimization_barrier((out_mine, pieces, under))
    normed_p, normed_q, cosine, sine, bias, gains = under
    strip_3 = from_tok(out_mine, dx=3)
    strips = [out_mine] + [from_tok(out_mine, dx=d) for d in (1, 2)]
    queries, kv = joint_projection(y[None], normed_p, normed_q, *pieces, cosine, sine, *gains)
    halo = from_previous_chip(kv)

    partial = prefix_attention(core[None], queries, prefix, scale)
    strips, partial, kv_sent = lax.optimization_barrier((strips, partial, kv))
    strips_other = [from_tok(s, dc=1) for s in strips]
    kv_got = from_tok(kv_sent, dc=1)[:, rows:]
    mine, others = suffix_attention(core[None], queries, kv, halo, partial, bias, scale)
    got = from_tok(others, dc=1)
    strip_3, mine = lax.optimization_barrier((strip_3, mine))
    strips.append(strip_3)
    strips_other.append(from_tok(strip_3, dc=1))
    projected = output_projection(x, core, mine, got, strips, strips_other)
    cache = in_core_order(core, kv[:, :rows], kv_got, 2)
    return (projected[None], cache[0][None], cache[1][None])


def solution(mesh):
    return jax.shard_map(
        per_device,
        mesh=mesh,
        in_specs=(
            P("grp", "tok", None),
            P("grp", "tok"),
            P("grp", "tok", None),
            P(),
            P(),
            P(),
            P(),
            P("tok", None),
            P("tok", None),
        ),
        out_specs=(P("grp", "tok", None), P("grp", "tok", None), P("grp", "tok", None)),
        check_vma=False,
    )
```

```python
import functools
import math

import jax
import jax.numpy as jnp
from jax import lax
from jax.experimental import pallas as pl
from jax.experimental.pallas import tpu as pltpu
from jax.sharding import PartitionSpec as P

NX, NZ, NC, NY = 4, 8, 2, 4

epsilon = 1e-06
theta_base = 1000000.0
floor_score = -1e30
VMEM_LIMIT = 56 * 1024 * 1024


def place(x, z, c):
    return (x * NZ + z) * NC + c


def from_tok(block, dx=0, dz=0, dc=0):
    route = [
        (place((x + dx) % NX, (z + dz) % NZ, (c + dc) % NC), place(x, z, c))
        for x in range(NX)
        for z in range(NZ)
        for c in range(NC)
    ]
    return lax.ppermute(block, "tok", route)


def from_grp(block, dy):
    return lax.ppermute(block, "grp", [((y + dy) % NY, y) for y in range(NY)])


def from_previous_chip(block):
    chips = NX * NZ
    route = [(p * NC + c, (p + 1) * NC + c) for p in range(chips - 1) for c in range(NC)]
    return lax.ppermute(block, "tok", route)


def in_core_order(core, mine, other, axis):
    first = jnp.where(core == 0, mine, other)
    second = jnp.where(core == 0, other, mine)
    return jnp.concatenate([first, second], axis=axis)


def norm_kernel(x_ref, own_ref, peer_ref, gain_ref, np_ref, nq_ref, scratch):
    half = own_ref.shape[0]
    gain = gain_ref[...].astype(jnp.float32)
    x = x_ref[0]
    for part, ref in enumerate((own_ref, peer_ref)):
        tokens = ref[...].astype(jnp.float32)
        mean = jnp.mean(tokens * tokens, axis=-1, keepdims=True)
        scratch[...] = (tokens * lax.rsqrt(mean + epsilon) * gain).astype(jnp.bfloat16)
        for j in range(NX):
            at = pl.multiple_of(((x + j) % NX) * 512, 512)
            np_ref[pl.ds(part * half, half), j * 256 : (j + 1) * 256] = scratch[:, pl.ds(at, 256)]
            at = pl.multiple_of(((x + j) % NX) * 512 + 256, 256)
            nq_ref[pl.ds(part * half, half), j * 256 : (j + 1) * 256] = scratch[:, pl.ds(at, 256)]


def input_norm(x, own, peer, gain):
    rows, width = own.shape
    out = jax.ShapeDtypeStruct((2 * rows, width // 2), jnp.bfloat16)
    vmem = pl.BlockSpec(memory_space=pltpu.VMEM)
    return pl.pallas_call(
        norm_kernel,
        out_shape=(out, out),
        in_specs=[pl.BlockSpec(memory_space=pltpu.SMEM), vmem, vmem, vmem],
        out_specs=(vmem, vmem),
        scratch_shapes=[pltpu.VMEM((rows, width), jnp.bfloat16)],
        compiler_params=pltpu.CompilerParams(vmem_limit_bytes=VMEM_LIMIT),
        name="input_norm",
    )(x, own, peer, gain)


def qkv_kernel(
    y_ref, np_ref, nq_ref, p0, p1, p2, p3, q0, q1, q2, q3, cos_ref, sin_ref, qg_ref, kg_ref,
    q_out, kv_out, acc
):
    step = pl.program_id(0)
    block = (y_ref[0] + step) % NY

    def dot(a, b):
        return jnp.dot(a, b, preferred_element_type=jnp.float32)

    for k, p in enumerate((p0, p1, p2, p3)):

        @pl.when(step == k)
        def _(p=p, k=k):
            total = dot(np_ref[...], p[...])
            for j, q in enumerate((q0, q1, q2, q3)):
                total = total + dot(
                    nq_ref[:, j * 256 : (j + 1) * 256], q[k * 256 : (k + 1) * 256, :]
                )
            acc[...] = total

    def turned(gain_ref, out):
        gain = gain_ref[...].astype(jnp.float32)
        for h in range(2):
            a = acc[:, h * 128 : (h + 1) * 128]
            mean = jnp.mean(a * a, axis=-1, keepdims=True)
            a = a * lax.rsqrt(mean + epsilon) * gain
            a = a * cos_ref[...] + pltpu.roll(a, 64, 1) * sin_ref[...]
            out[0, :, h * 128 : (h + 1) * 128] = a.astype(jnp.bfloat16)

    @pl.when(block < 2)
    def _():
        turned(qg_ref, q_out)

    @pl.when(block == 2)
    def _():
        turned(kg_ref, kv_out)

    @pl.when(block == 3)
    def _():
        kv_out[0] = acc[...].astype(jnp.bfloat16)


def query_block(i, y_ref):
    block = (y_ref[0] + i) % NY
    return jnp.where(block < 2, block, jnp.where(i >= block - 1, 1, 0)), 0, 0


def key_value_block(i, y_ref):
    block = (y_ref[0] + i) % NY
    return jnp.where(block >= 2, block - 2, jnp.where(i >= block + 1, 1, 0)), 0, 0


def joint_projection(y, normed_p, normed_q, p, q, cosine, sine, query_gain, key_gain):
    rows = normed_p.shape[0]
    whole = lambda a: pl.BlockSpec(a.shape, lambda i, y_ref: (0,) * a.ndim)
    args = [normed_p, normed_q, *p, *q, cosine, sine, query_gain, key_gain]
    out = jax.ShapeDtypeStruct((2, rows, 256), jnp.bfloat16)
    return pl.pallas_call(
        qkv_kernel,
        out_shape=(out, out),
        grid_spec=pltpu.PrefetchScalarGridSpec(
            num_scalar_prefetch=1,
            grid=(NY,),
            in_specs=[whole(a) for a in args],
            out_specs=(
                pl.BlockSpec((1, rows, 256), query_block),
                pl.BlockSpec((1, rows, 256), key_value_block),
            ),
            scratch_shapes=[pltpu.VMEM((rows, 256), jnp.float32)],
        ),
        compiler_params=pltpu.CompilerParams(
            dimension_semantics=("arbitrary",), vmem_limit_bytes=VMEM_LIMIT
        ),
        cost_estimate=pl.CostEstimate(
            flops=2 * rows * 2048 * 1024, transcendentals=0, bytes_accessed=8 << 20
        ),
        name="joint_projection",
    )(y, *args)


LANES = (((1,), (1,)), ((), ()))


def fold(op, blocks):
    return functools.reduce(
        op, [b[:, i : i + 128] for b in blocks for i in range(0, b.shape[1], 128)]
    )


def row_max(blocks):
    return jnp.max(fold(jnp.maximum, blocks), axis=-1, keepdims=True)


def prefix_kernel(scale, core_ref, q_ref, k_ref, v_ref, acc_ref, stat_ref):
    rows, step = 256, 512
    starts = range(0, k_ref.shape[0], step)
    for r in range(0, q_ref.shape[1], rows):
        for h in range(2):
            q = q_ref[0, r : r + rows, h * 128 : (h + 1) * 128]
            scores = [
                lax.dot_general(
                    q, k_ref[i : i + step, :], LANES, preferred_element_type=jnp.float32
                )
                for i in starts
            ]
            top = row_max(scores)
            total = jnp.zeros(q.shape, jnp.float32)
            acc = jnp.zeros(q.shape, jnp.float32)
            for s, i in zip(scores, starts):
                w = jnp.exp2((s - top) * scale)
                total = total + fold(jnp.add, [w])
                acc = acc + jnp.dot(
                    w.astype(jnp.bfloat16),
                    v_ref[i : i + step, :],
                    preferred_element_type=jnp.float32,
                )
            acc_ref[h, r : r + rows, :] = acc
            stat_ref[h, r : r + rows, 0:1] = top
            stat_ref[h, r : r + rows, 1:2] = jnp.sum(total, axis=-1, keepdims=True)


def prefix_attention(core, qkv, prefix, scale):
    rows = qkv.shape[1]
    keys = prefix.shape[0]
    out = jax.ShapeDtypeStruct((4, rows, 128), jnp.float32)
    pair = pl.BlockSpec((2, rows, 128), lambda g, c: (g, 0, 0))
    return pl.pallas_call(
        functools.partial(prefix_kernel, scale),
        out_shape=(out, out),
        grid_spec=pltpu.PrefetchScalarGridSpec(
            num_scalar_prefetch=1,
            grid=(2,),
            in_specs=[
                pl.BlockSpec((1, rows, 256), lambda g, c: (g, 0, 0)),
                pl.BlockSpec((keys, 128), lambda g, c: (0, 2 * c[0] + g)),
                pl.BlockSpec((keys, 128), lambda g, c: (0, 4 + 2 * c[0] + g)),
            ],
            out_specs=(pair, pair),
        ),
        compiler_params=pltpu.CompilerParams(
            dimension_semantics=("arbitrary",), vmem_limit_bytes=VMEM_LIMIT
        ),
        cost_estimate=pl.CostEstimate(
            flops=4 * 4 * rows * keys * 128, transcendentals=4 * rows * keys, bytes_accessed=4 << 20
        ),
        name="prefix_attention",
    )(core, qkv, prefix, prefix)


def suffix_kernel(
    scale, core_ref, q_ref, ko_ref, vo_ref, kh_ref, vh_ref, acc_ref, stat_ref, bias_ref,
    own_ref, peer_ref
):
    core = core_ref[0]
    rows = own_ref.shape[0]
    zero = pl.ds(pl.multiple_of(core * rows, rows), rows)
    one = pl.ds(pl.multiple_of((1 - core) * rows, rows), rows)
    for r, out_ref in enumerate((own_ref, peer_ref)):
        block = slice(r * rows, (r + 1) * rows)
        third = [jnp.where(core == r, h[0, block, :], o[0, block, :])
                 for h, o in ((kh_ref, ko_ref), (vh_ref, vo_ref))]
        keys = [kh_ref[0, one, :], ko_ref[0, zero, :], third[0]]
        values = [vh_ref[0, one, :], vo_ref[0, zero, :], third[1]]
        for h in range(2):
            q = q_ref[0, block, h * 128 : (h + 1) * 128]
            scores = [
                lax.dot_general(q, k, LANES, preferred_element_type=jnp.float32)
                + bias_ref[r, :, i * rows : (i + 1) * rows].astype(jnp.float32)
                for i, k in enumerate(keys)
            ]
            before = stat_ref[h, block, 0:1]
            top = jnp.maximum(before, row_max(scores))
            shrink = jnp.exp2((before - top) * scale)
            weights = [jnp.exp2((s - top) * scale) for s in scores]
            total = jnp.sum(fold(jnp.add, weights), axis=-1, keepdims=True)
            total = stat_ref[h, block, 1:2] * shrink + total
            acc = acc_ref[h, block, :] * shrink
            for w, v in zip(weights, values):
                acc = acc + jnp.dot(w.astype(jnp.bfloat16), v, preferred_element_type=jnp.float32)
            out_ref[:, h * 128 : (h + 1) * 128] = (acc / total).astype(jnp.bfloat16)


def suffix_attention(core, queries, own, halo, partial, bias, scale):
    rows = queries.shape[1]
    pair = pl.BlockSpec((2, rows, 128), lambda g, c: (g, 0, 0))
    head = lambda block: pl.BlockSpec((1, rows, 128), lambda g, c: (block, 0, g))
    out = jax.ShapeDtypeStruct((rows // 2, 512), jnp.bfloat16)
    out_spec = pl.BlockSpec((rows // 2, 256), lambda g, c: (0, g))
    return pl.pallas_call(
        functools.partial(suffix_kernel, scale),
        out_shape=(out, out),
        grid_spec=pltpu.PrefetchScalarGridSpec(
            num_scalar_prefetch=1,
            grid=(2,),
            in_specs=[
                pl.BlockSpec((1, rows, 256), lambda g, c: (g, 0, 0)),
                head(0),
                head(1),
                head(0),
                head(1),
                pair,
                pair,
                pl.BlockSpec(bias.shape, lambda g, c: (0, 0, 0)),
            ],
            out_specs=(out_spec, out_spec),
        ),
        compiler_params=pltpu.CompilerParams(
            dimension_semantics=("arbitrary",), vmem_limit_bytes=VMEM_LIMIT
        ),
        cost_estimate=pl.CostEstimate(
            flops=4 * 4 * rows * 768 * 128, transcendentals=4 * rows * 768, bytes_accessed=4 << 20
        ),
        name="suffix_attention",
    )(core, queries, own, own, halo, halo, *partial, bias)


def out_kernel(place_ref, mine_ref, other_ref, *refs):
    *weights, out_ref, heads = refs
    x, core = place_ref[0], place_ref[1]
    heads[:, pl.ds(pl.multiple_of(core * 512, 512), 512)] = mine_ref[...]
    heads[:, pl.ds(pl.multiple_of((1 - core) * 512, 512), 512)] = other_ref[...]
    for c, strips in ((core, weights[:NX]), (1 - core, weights[NX:])):
        total = jnp.zeros((mine_ref.shape[0], 1024), jnp.float32)
        for j, strip in enumerate(strips):
            at = pl.multiple_of(((x + j) % NX) * 256, 256)
            total = total + jnp.dot(
                heads[:, pl.ds(at, 256)], strip[...], preferred_element_type=jnp.float32
            )
        out_ref[:, pl.ds(pl.multiple_of(c * 1024, 1024), 1024)] = total.astype(jnp.bfloat16)


def output_projection(x, core, mine, other, strips, strips_other):
    rows = mine.shape[0]
    vmem = pl.BlockSpec(memory_space=pltpu.VMEM)
    args = [mine, other, *strips, *strips_other]
    return pl.pallas_call(
        out_kernel,
        out_shape=jax.ShapeDtypeStruct((rows, 2048), jnp.bfloat16),
        in_specs=[pl.BlockSpec(memory_space=pltpu.SMEM)] + [vmem] * len(args),
        out_specs=vmem,
        scratch_shapes=[pltpu.VMEM((rows, 1024), jnp.bfloat16)],
        compiler_params=pltpu.CompilerParams(vmem_limit_bytes=VMEM_LIMIT),
        cost_estimate=pl.CostEstimate(
            flops=2 * rows * 1024 * 2048, transcendentals=0, bytes_accessed=6 << 20
        ),
        name="output_projection",
    )(jnp.stack([x, core]), *args)


GROUP_ZC = [[place(x, z, c) for z in range(NZ) for c in range(NC)] for x in range(NX)]


def per_device(
    hidden_in, doc_ids, prefix_kv, prefix_owner, norm_gain, query_gain, key_norm_gain, w_qkv, w_out
):
    rows = hidden_in.shape[1]
    head_dim = query_gain.shape[0]
    prefix_len = prefix_kv.shape[1] * lax.axis_size("tok")
    scale = head_dim ** (-0.5) * math.log2(math.e)
    place_tok = lax.axis_index("tok")
    y = lax.axis_index("grp")
    x, z, core = place_tok // (NZ * NC), (place_tok // NC) % NZ, place_tok % NC

    own = hidden_in[0]
    out_strip = lax.all_gather(w_out, "tok", axis_index_groups=GROUP_ZC, tiled=True)
    owners = [prefix_kv[0]] + [from_grp(prefix_kv[0], d) for d in range(1, NY)]
    owner = (prefix_owner[y] - y) % NY

    def columns(c):
        start = jnp.where(y < 2, 512 * c + 256 * y, 512 * y + 256 * c)
        return lax.dynamic_slice(w_qkv, (jnp.int32(0), start), (w_qkv.shape[0], 256))

    marks = (doc_ids + 1).astype(jnp.bfloat16)
    first = jnp.concatenate(
        [
            jnp.concatenate([columns(0), columns(1)], axis=1),
            jnp.pad(marks, ((0, 7), (0, 256))),
        ],
        axis=0,
    )
    both = lax.all_gather(first, "tok", axis_index_groups=GROUP_ZC)
    peer = from_tok(own, dc=1)
    both, owners, peer, query_gain, key_norm_gain = lax.optimization_barrier(
        (both, owners, peer, query_gain, key_norm_gain)
    )

    marks_x = both[:, 32, :256]
    strip = lax.dynamic_slice_in_dim(both[:, :32], core * 256, 256, 2).reshape(512, 256)
    prefix_rows = lax.dynamic_index_in_dim(jnp.stack(owners), owner, 0, keepdims=False)
    p_own = jnp.concatenate(
        [strip[:256]]
        + [prefix_rows[:, i * 256 : (i + 1) * 256] for i in range(4)]
        + [jnp.pad(marks_x[14:], ((0, 6), (0, 0)))]
    )
    q_own = jnp.concatenate([strip[256:], jnp.zeros((8, 256), jnp.bfloat16)])
    p_all = [p_own] + [from_tok(p_own, dx=d) for d in (2, 1, 3)]
    p_all = [p_all[0], p_all[2], p_all[1], p_all[3]]
    q_all = [q_own] + [from_grp(q_own, d) for d in range(1, NY)]
    p_all, q_all = lax.optimization_barrier((p_all, q_all))

    p0 = jnp.concatenate([p[:256] for p in p_all])
    q0 = jnp.concatenate([q[:256] for q in q_all])
    prefix_part = jnp.concatenate(
        [
            jnp.concatenate([p[256 + 32 * i : 288 + 32 * i] for i in range(4)], axis=1)
            for p in p_all
        ]
    )
    p2 = from_grp(p0, 2)
    p1, p3 = from_grp(p0, 1), from_grp(p0, 3)
    q1, q3 = from_tok(q0, dx=1), from_tok(q0, dx=3)
    q2 = from_tok(q0, dx=2)
    prefix = lax.all_gather(prefix_part, "tok", axis_index_groups=GROUP_ZC, tiled=True)

    own, peer, norm_gain, p1 = lax.optimization_barrier((own, peer, norm_gain, p1))
    normed_p, normed_q = input_norm(x[None], own, peer, norm_gain[None, :])
    marks_left = jnp.where(x > 0, p_all[3][384:386], 0)
    near = lax.dynamic_slice_in_dim(
        jnp.concatenate([marks_left, marks_x]).astype(jnp.float32), 2 * z, 4, 0
    )
    row = lax.broadcasted_iota(jnp.int32, (rows, rows), 0)
    column = lax.broadcasted_iota(jnp.int32, (rows, rows), 1)
    bias, offset = [], []
    for part in range(2):
        upper = (core + part) % 2
        marks_q = lax.dynamic_index_in_dim(near, 2 + upper, 0, keepdims=False)[:, None]
        third = jnp.where(upper == 0, near[0], near[3])
        counted = 0
        for keys, whole in ((near[1], True), (near[2], upper == 1), (third, upper == 0)):
            same = marks_q == keys[None, :]
            seen = same & ((column <= row) | whole)
            bias.append(jnp.where(seen, 0.0, floor_score).astype(jnp.bfloat16))
            counted += jnp.sum((same & ((column < row) | whole)).astype(jnp.int32), axis=1)
        offset.append(counted)
    bias = jnp.stack(
        [jnp.concatenate(bias[:3], axis=1), jnp.concatenate(bias[3:], axis=1)]
    )
    offset = jnp.concatenate(offset)
    token_positions = (prefix_len + offset).astype(jnp.float32)
    half_width = head_dim // 2
    freqs = theta_base ** (-jnp.arange(half_width, dtype=jnp.float32) / half_width)
    angles = token_positions[:, None] * freqs[None, :]
    cosine, sine = jnp.cos(angles), jnp.sin(angles)
    cosine = jnp.concatenate([cosine, cosine], axis=1)
    sine = jnp.concatenate([-sine, sine], axis=1)
    gains = (query_gain[None, :], key_norm_gain[None, :])

    under = (normed_p, normed_q, cosine, sine, bias, gains)
    pieces = ([p0, p1, p2, p3], [q0, q1, q2, q3])

    out_mine = lax.dynamic_slice_in_dim(out_strip, core * 1024, 1024, 1)
    out_mine, pieces, under = lax.optimization_barrier((out_mine, pieces, under))
    normed_p, normed_q, cosine, sine, bias, gains = under
    strip_3 = from_tok(out_mine, dx=3)
    strips = [out_mine] + [from_tok(out_mine, dx=d) for d in (1, 2)]
    queries, kv = joint_projection(y[None], normed_p, normed_q, *pieces, cosine, sine, *gains)
    halo = from_previous_chip(kv)

    partial = prefix_attention(core[None], queries, prefix, scale)
    strips, partial, kv_sent = lax.optimization_barrier((strips, partial, kv))
    strips_other = [from_tok(s, dc=1) for s in strips]
    kv_got = from_tok(kv_sent, dc=1)[:, rows:]
    mine, others = suffix_attention(core[None], queries, kv, halo, partial, bias, scale)
    got = from_tok(others, dc=1)
    strip_3, mine = lax.optimization_barrier((strip_3, mine))
    strips.append(strip_3)
    strips_other.append(from_tok(strip_3, dc=1))
    projected = output_projection(x, core, mine, got, strips, strips_other)
    cache = in_core_order(core, kv[:, :rows], kv_got, 2)
    return (projected[None], cache[0][None], cache[1][None])


def solution(mesh):
    return jax.shard_map(
        per_device,
        mesh=mesh,
        in_specs=(
            P("grp", "tok", None),
            P("grp", "tok"),
            P("grp", "tok", None),
            P(),
            P(),
            P(),
            P(),
            P("tok", None),
            P("tok", None),
        ),
        out_specs=(P("grp", "tok", None), P("grp", "tok", None), P("grp", "tok", None)),
        check_vma=False,
    )
```

```python
import functools
import math

import jax
import jax.numpy as jnp
from jax import lax
from jax.experimental import pallas as pl
from jax.experimental.pallas import tpu as pltpu
from jax.sharding import PartitionSpec as P

NX, NZ, NC, NY = 4, 8, 2, 4

epsilon = 1e-06
theta_base = 1000000.0
floor_score = -1e30
VMEM_LIMIT = 56 * 1024 * 1024


def place(x, z, c):
    return (x * NZ + z) * NC + c


def from_tok(block, dx=0, dz=0, dc=0):
    route = [
        (place((x + dx) % NX, (z + dz) % NZ, (c + dc) % NC), place(x, z, c))
        for x in range(NX)
        for z in range(NZ)
        for c in range(NC)
    ]
    return lax.ppermute(block, "tok", route)


def from_grp(block, dy):
    return lax.ppermute(block, "grp", [((y + dy) % NY, y) for y in range(NY)])


def from_previous_chip(block):
    chips = NX * NZ
    route = [(p * NC + c, (p + 1) * NC + c) for p in range(chips - 1) for c in range(NC)]
    return lax.ppermute(block, "tok", route)


def in_core_order(core, mine, other, axis):
    first = jnp.where(core == 0, mine, other)
    second = jnp.where(core == 0, other, mine)
    return jnp.concatenate([first, second], axis=axis)


def norm_kernel(x_ref, own_ref, peer_ref, gain_ref, np_ref, nq_ref, scratch):
    half = own_ref.shape[0]
    gain = gain_ref[...].astype(jnp.float32)
    x = x_ref[0]
    for part, ref in enumerate((own_ref, peer_ref)):
        tokens = ref[...].astype(jnp.float32)
        mean = jnp.mean(tokens * tokens, axis=-1, keepdims=True)
        scratch[...] = (tokens * lax.rsqrt(mean + epsilon) * gain).astype(jnp.bfloat16)
        for j in range(NX):
            at = pl.multiple_of(((x + j) % NX) * 512, 512)
            np_ref[pl.ds(part * half, half), j * 256 : (j + 1) * 256] = scratch[:, pl.ds(at, 256)]
            at = pl.multiple_of(((x + j) % NX) * 512 + 256, 256)
            nq_ref[pl.ds(part * half, half), j * 256 : (j + 1) * 256] = scratch[:, pl.ds(at, 256)]


def input_norm(x, own, peer, gain):
    rows, width = own.shape
    out = jax.ShapeDtypeStruct((2 * rows, width // 2), jnp.bfloat16)
    vmem = pl.BlockSpec(memory_space=pltpu.VMEM)
    return pl.pallas_call(
        norm_kernel,
        out_shape=(out, out),
        in_specs=[pl.BlockSpec(memory_space=pltpu.SMEM), vmem, vmem, vmem],
        out_specs=(vmem, vmem),
        scratch_shapes=[pltpu.VMEM((rows, width), jnp.bfloat16)],
        compiler_params=pltpu.CompilerParams(vmem_limit_bytes=VMEM_LIMIT),
        name="input_norm",
    )(x, own, peer, gain)


def qkv_kernel(
    y_ref, np_ref, nq_ref, p0, p1, p2, p3, q0, q1, q2, q3, cos_ref, sin_ref, qg_ref, kg_ref,
    q_out, kv_out, acc, b1, b2, b3, sems
):
    step = pl.program_id(0)
    block = (y_ref[0] + step) % NY
    copies = [
        pltpu.make_async_copy(p, b, sems.at[i])
        for i, (p, b) in enumerate(((p1, b1), (p2, b2), (p3, b3)))
    ]

    @pl.when(step == 0)
    def _():
        for copy in copies:
            copy.start()

    def dot(a, b):
        return jnp.dot(a, b, preferred_element_type=jnp.float32)

    for k, p in enumerate((p0, b1, b2, b3)):

        @pl.when(step == k)
        def _(p=p, k=k):
            if k > 0:
                copies[k - 1].wait()
            total = dot(np_ref[...], p[...])
            for j, q in enumerate((q0, q1, q2, q3)):
                total = total + dot(nq_ref[:, j * 256 : (j + 1) * 256], q[...])
            acc[...] = total

    def turned(gain_ref, out):
        gain = gain_ref[...].astype(jnp.float32)
        for h in range(2):
            a = acc[:, h * 128 : (h + 1) * 128]
            mean = jnp.mean(a * a, axis=-1, keepdims=True)
            a = a * lax.rsqrt(mean + epsilon) * gain
            a = a * cos_ref[...] + pltpu.roll(a, 64, 1) * sin_ref[...]
            out[0, :, h * 128 : (h + 1) * 128] = a.astype(jnp.bfloat16)

    @pl.when(block < 2)
    def _():
        turned(qg_ref, q_out)

    @pl.when(block == 2)
    def _():
        turned(kg_ref, kv_out)

    @pl.when(block == 3)
    def _():
        kv_out[0] = acc[...].astype(jnp.bfloat16)


def query_block(i, y_ref):
    block = (y_ref[0] + i) % NY
    return jnp.where(block < 2, block, jnp.where(i >= block - 1, 1, 0)), 0, 0


def key_value_block(i, y_ref):
    block = (y_ref[0] + i) % NY
    return jnp.where(block >= 2, block - 2, jnp.where(i >= block + 1, 1, 0)), 0, 0


def joint_projection(y, normed_p, normed_q, p, q, cosine, sine, query_gain, key_gain):
    rows = normed_p.shape[0]
    whole = lambda a: pl.BlockSpec(a.shape, lambda i, y_ref: (0,) * a.ndim)
    args = [normed_p, normed_q, *p, *q, cosine, sine, query_gain, key_gain]
    out = jax.ShapeDtypeStruct((2, rows, 256), jnp.bfloat16)
    return pl.pallas_call(
        qkv_kernel,
        out_shape=(out, out),
        grid_spec=pltpu.PrefetchScalarGridSpec(
            num_scalar_prefetch=1,
            grid=(NY,),
            in_specs=[whole(normed_p), whole(normed_q), whole(p[0])]
            + [pl.BlockSpec(memory_space=pl.ANY)] * 3
            + [pl.BlockSpec((256, 256), lambda i, y_ref: (i, 0))] * 4
            + [whole(a) for a in args[-4:]],
            out_specs=(
                pl.BlockSpec((1, rows, 256), query_block),
                pl.BlockSpec((1, rows, 256), key_value_block),
            ),
            scratch_shapes=[pltpu.VMEM((rows, 256), jnp.float32)]
            + [pltpu.VMEM((1024, 256), jnp.bfloat16)] * 3
            + [pltpu.SemaphoreType.DMA((3,))],
        ),
        compiler_params=pltpu.CompilerParams(
            dimension_semantics=("arbitrary",), vmem_limit_bytes=VMEM_LIMIT
        ),
        cost_estimate=pl.CostEstimate(
            flops=2 * rows * 2048 * 1024, transcendentals=0, bytes_accessed=8 << 20
        ),
        name="joint_projection",
    )(y, *args)


LANES = (((1,), (1,)), ((), ()))


def fold(op, blocks):
    return functools.reduce(
        op, [b[:, i : i + 128] for b in blocks for i in range(0, b.shape[1], 128)]
    )


def row_max(blocks):
    return jnp.max(fold(jnp.maximum, blocks), axis=-1, keepdims=True)


def prefix_kernel(scale, core_ref, q_ref, k_ref, v_ref, acc_ref, stat_ref):
    rows, step = 256, 512
    starts = range(0, k_ref.shape[0], step)
    for r in range(0, q_ref.shape[1], rows):
        for h in range(2):
            q = q_ref[0, r : r + rows, h * 128 : (h + 1) * 128]
            scores = [
                lax.dot_general(
                    q, k_ref[i : i + step, :], LANES, preferred_element_type=jnp.float32
                )
                for i in starts
            ]
            top = row_max(scores)
            total = jnp.zeros(q.shape, jnp.float32)
            acc = jnp.zeros(q.shape, jnp.float32)
            for s, i in zip(scores, starts):
                w = jnp.exp2((s - top) * scale)
                total = total + fold(jnp.add, [w])
                acc = acc + jnp.dot(
                    w.astype(jnp.bfloat16),
                    v_ref[i : i + step, :],
                    preferred_element_type=jnp.float32,
                )
            acc_ref[h, r : r + rows, :] = acc
            stat_ref[h, r : r + rows, 0:1] = top
            stat_ref[h, r : r + rows, 1:2] = jnp.sum(total, axis=-1, keepdims=True)


def prefix_attention(core, qkv, prefix, scale):
    rows = qkv.shape[1]
    keys = prefix.shape[0]
    out = jax.ShapeDtypeStruct((4, rows, 128), jnp.float32)
    pair = pl.BlockSpec((2, rows, 128), lambda g, c: (g, 0, 0))
    return pl.pallas_call(
        functools.partial(prefix_kernel, scale),
        out_shape=(out, out),
        grid_spec=pltpu.PrefetchScalarGridSpec(
            num_scalar_prefetch=1,
            grid=(2,),
            in_specs=[
                pl.BlockSpec((1, rows, 256), lambda g, c: (g, 0, 0)),
                pl.BlockSpec((keys, 128), lambda g, c: (0, 2 * c[0] + g)),
                pl.BlockSpec((keys, 128), lambda g, c: (0, 4 + 2 * c[0] + g)),
            ],
            out_specs=(pair, pair),
        ),
        compiler_params=pltpu.CompilerParams(
            dimension_semantics=("arbitrary",), vmem_limit_bytes=VMEM_LIMIT
        ),
        cost_estimate=pl.CostEstimate(
            flops=4 * 4 * rows * keys * 128, transcendentals=4 * rows * keys, bytes_accessed=4 << 20
        ),
        name="prefix_attention",
    )(core, qkv, prefix, prefix)


def suffix_kernel(
    scale, core_ref, q_ref, ko_ref, vo_ref, kh_ref, vh_ref, acc_ref, stat_ref, bias_ref,
    own_ref, peer_ref
):
    core = core_ref[0]
    rows = own_ref.shape[0]
    zero = pl.ds(pl.multiple_of(core * rows, rows), rows)
    one = pl.ds(pl.multiple_of((1 - core) * rows, rows), rows)
    for r, out_ref in enumerate((own_ref, peer_ref)):
        block = slice(r * rows, (r + 1) * rows)
        third = [jnp.where(core == r, h[0, block, :], o[0, block, :])
                 for h, o in ((kh_ref, ko_ref), (vh_ref, vo_ref))]
        keys = [kh_ref[0, one, :], ko_ref[0, zero, :], third[0]]
        values = [vh_ref[0, one, :], vo_ref[0, zero, :], third[1]]
        for h in range(2):
            q = q_ref[0, block, h * 128 : (h + 1) * 128]
            scores = [
                lax.dot_general(q, k, LANES, preferred_element_type=jnp.float32)
                + bias_ref[r, :, i * rows : (i + 1) * rows].astype(jnp.float32)
                for i, k in enumerate(keys)
            ]
            before = stat_ref[h, block, 0:1]
            top = jnp.maximum(before, row_max(scores))
            shrink = jnp.exp2((before - top) * scale)
            weights = [jnp.exp2((s - top) * scale) for s in scores]
            total = jnp.sum(fold(jnp.add, weights), axis=-1, keepdims=True)
            total = stat_ref[h, block, 1:2] * shrink + total
            acc = acc_ref[h, block, :] * shrink
            for w, v in zip(weights, values):
                acc = acc + jnp.dot(w.astype(jnp.bfloat16), v, preferred_element_type=jnp.float32)
            out_ref[:, h * 128 : (h + 1) * 128] = (acc / total).astype(jnp.bfloat16)


def suffix_attention(core, queries, own, halo, partial, bias, scale):
    rows = queries.shape[1]
    pair = pl.BlockSpec((2, rows, 128), lambda g, c: (g, 0, 0))
    head = lambda block: pl.BlockSpec((1, rows, 128), lambda g, c: (block, 0, g))
    out = jax.ShapeDtypeStruct((rows // 2, 512), jnp.bfloat16)
    out_spec = pl.BlockSpec((rows // 2, 256), lambda g, c: (0, g))
    return pl.pallas_call(
        functools.partial(suffix_kernel, scale),
        out_shape=(out, out),
        grid_spec=pltpu.PrefetchScalarGridSpec(
            num_scalar_prefetch=1,
            grid=(2,),
            in_specs=[
                pl.BlockSpec((1, rows, 256), lambda g, c: (g, 0, 0)),
                head(0),
                head(1),
                head(0),
                head(1),
                pair,
                pair,
                pl.BlockSpec(bias.shape, lambda g, c: (0, 0, 0)),
            ],
            out_specs=(out_spec, out_spec),
        ),
        compiler_params=pltpu.CompilerParams(
            dimension_semantics=("arbitrary",), vmem_limit_bytes=VMEM_LIMIT
        ),
        cost_estimate=pl.CostEstimate(
            flops=4 * 4 * rows * 768 * 128, transcendentals=4 * rows * 768, bytes_accessed=4 << 20
        ),
        name="suffix_attention",
    )(core, queries, own, own, halo, halo, *partial, bias)


def out_kernel(place_ref, mine_ref, other_ref, *refs):
    *weights, out_ref, heads = refs
    x, core = place_ref[0], place_ref[1]
    heads[:, pl.ds(pl.multiple_of(core * 512, 512), 512)] = mine_ref[...]
    heads[:, pl.ds(pl.multiple_of((1 - core) * 512, 512), 512)] = other_ref[...]
    for c, strips in ((core, weights[:NX]), (1 - core, weights[NX:])):
        total = jnp.zeros((mine_ref.shape[0], 1024), jnp.float32)
        for j, strip in enumerate(strips):
            at = pl.multiple_of(((x + j) % NX) * 256, 256)
            total = total + jnp.dot(
                heads[:, pl.ds(at, 256)], strip[...], preferred_element_type=jnp.float32
            )
        out_ref[:, pl.ds(pl.multiple_of(c * 1024, 1024), 1024)] = total.astype(jnp.bfloat16)


def output_projection(place_xc, mine, other, strips, strips_other):
    rows = mine.shape[0]
    vmem = pl.BlockSpec(memory_space=pltpu.VMEM)
    args = [mine, other, *strips, *strips_other]
    return pl.pallas_call(
        out_kernel,
        out_shape=jax.ShapeDtypeStruct((rows, 2048), jnp.bfloat16),
        in_specs=[pl.BlockSpec(memory_space=pltpu.SMEM)] + [vmem] * len(args),
        out_specs=vmem,
        scratch_shapes=[pltpu.VMEM((rows, 1024), jnp.bfloat16)],
        compiler_params=pltpu.CompilerParams(vmem_limit_bytes=VMEM_LIMIT),
        cost_estimate=pl.CostEstimate(
            flops=2 * rows * 1024 * 2048, transcendentals=0, bytes_accessed=6 << 20
        ),
        name="output_projection",
    )(place_xc, *args)


GROUP_ZC = [[place(x, z, c) for z in range(NZ) for c in range(NC)] for x in range(NX)]


def per_device(
    hidden_in, doc_ids, prefix_kv, prefix_owner, norm_gain, query_gain, key_norm_gain, w_qkv, w_out
):
    rows = hidden_in.shape[1]
    head_dim = query_gain.shape[0]
    prefix_len = prefix_kv.shape[1] * lax.axis_size("tok")
    scale = head_dim ** (-0.5) * math.log2(math.e)
    place_tok = lax.axis_index("tok")
    y = lax.axis_index("grp")
    x, z, core = place_tok // (NZ * NC), (place_tok // NC) % NZ, place_tok % NC

    own = hidden_in[0]
    out_strip = lax.all_gather(w_out, "tok", axis_index_groups=GROUP_ZC, tiled=True)
    owners = [prefix_kv[0]] + [from_grp(prefix_kv[0], d) for d in range(1, NY)]
    owner = (prefix_owner[y] - y) % NY

    def columns(c):
        start = jnp.where(y < 2, 512 * c + 256 * y, 512 * y + 256 * c)
        return lax.dynamic_slice(w_qkv, (jnp.int32(0), start), (w_qkv.shape[0], 256))

    marks = (doc_ids + 1).astype(jnp.bfloat16)
    first = jnp.concatenate(
        [
            jnp.concatenate([columns(0), columns(1)], axis=1),
            jnp.pad(marks, ((0, 7), (0, 256))),
        ],
        axis=0,
    )
    both = lax.all_gather(first, "tok", axis_index_groups=GROUP_ZC)
    peer = from_tok(own, dc=1)
    both, owners, peer, query_gain, key_norm_gain = lax.optimization_barrier(
        (both, owners, peer, query_gain, key_norm_gain)
    )

    marks_x = both[:, 32, :256]
    strip = lax.dynamic_slice_in_dim(both[:, :32], core * 256, 256, 2).reshape(512, 256)
    prefix_rows = lax.dynamic_index_in_dim(jnp.stack(owners), owner, 0, keepdims=False)
    p_own = jnp.concatenate(
        [strip[:256]]
        + [prefix_rows[:, i * 256 : (i + 1) * 256] for i in range(4)]
        + [jnp.pad(marks_x[14:], ((0, 6), (0, 0)))]
    )
    q_own = jnp.concatenate([strip[256:], jnp.zeros((8, 256), jnp.bfloat16)])
    p_all = [p_own] + [from_tok(p_own, dx=d) for d in (2, 1, 3)]
    p_all = [p_all[0], p_all[2], p_all[1], p_all[3]]
    q_all = [q_own] + [from_grp(q_own, d) for d in range(1, NY)]
    p_all, q_all = lax.optimization_barrier((p_all, q_all))

    p0 = jnp.concatenate([p[:256] for p in p_all])
    q0 = jnp.concatenate([q[:256] for q in q_all])
    prefix_part = jnp.concatenate(
        [
            jnp.concatenate([p[256 + 32 * i : 288 + 32 * i] for i in range(4)], axis=1)
            for p in p_all
        ]
    )
    p2 = from_grp(p0, 2)
    p1, p3 = from_grp(p0, 1), from_grp(p0, 3)
    q1, q3 = from_tok(q0, dx=1), from_tok(q0, dx=3)
    q2 = from_tok(q0, dx=2)
    prefix = lax.all_gather(prefix_part, "tok", axis_index_groups=GROUP_ZC, tiled=True)

    own, peer, norm_gain, p1 = lax.optimization_barrier((own, peer, norm_gain, p1))
    normed_p, normed_q = input_norm(x[None], own, peer, norm_gain[None, :])
    marks_left = jnp.where(x > 0, p_all[3][384:386], 0)
    near = lax.dynamic_slice_in_dim(
        jnp.concatenate([marks_left, marks_x]).astype(jnp.float32), 2 * z, 4, 0
    )
    row = lax.broadcasted_iota(jnp.int32, (rows, rows), 0)
    column = lax.broadcasted_iota(jnp.int32, (rows, rows), 1)
    bias, offset = [], []
    for part in range(2):
        upper = (core + part) % 2
        marks_q = lax.dynamic_index_in_dim(near, 2 + upper, 0, keepdims=False)[:, None]
        third = jnp.where(upper == 0, near[0], near[3])
        counted = 0
        for keys, whole in ((near[1], True), (near[2], upper == 1), (third, upper == 0)):
            same = marks_q == keys[None, :]
            seen = same & ((column <= row) | whole)
            bias.append(jnp.where(seen, 0.0, floor_score).astype(jnp.bfloat16))
            counted += jnp.sum((same & ((column < row) | whole)).astype(jnp.int32), axis=1)
        offset.append(counted)
    bias = jnp.stack(
        [jnp.concatenate(bias[:3], axis=1), jnp.concatenate(bias[3:], axis=1)]
    )
    offset = jnp.concatenate(offset)
    token_positions = (prefix_len + offset).astype(jnp.float32)
    half_width = head_dim // 2
    freqs = theta_base ** (-jnp.arange(half_width, dtype=jnp.float32) / half_width)
    angles = token_positions[:, None] * freqs[None, :]
    cosine, sine = jnp.cos(angles), jnp.sin(angles)
    cosine = jnp.concatenate([cosine, cosine], axis=1)
    sine = jnp.concatenate([-sine, sine], axis=1)
    gains = (query_gain[None, :], key_norm_gain[None, :])

    under = (normed_p, normed_q, cosine, sine, bias, gains)
    pieces = ([p0, p1, p2, p3], [q0, q1, q2, q3])
    place_xc = jnp.stack([x, core])

    out_mine = lax.dynamic_slice_in_dim(out_strip, core * 1024, 1024, 1)
    out_mine, pieces, under, place_xc = lax.optimization_barrier(
        (out_mine, pieces, under, place_xc)
    )
    normed_p, normed_q, cosine, sine, bias, gains = under
    strip_3 = from_tok(out_mine, dx=3)
    strips = [out_mine] + [from_tok(out_mine, dx=d) for d in (1, 2)]
    queries, kv = joint_projection(y[None], normed_p, normed_q, *pieces, cosine, sine, *gains)
    halo = from_previous_chip(kv)

    partial = prefix_attention(core[None], queries, prefix, scale)
    strips, partial, kv_sent = lax.optimization_barrier((strips, partial, kv))
    strips_other = [from_tok(s, dc=1) for s in strips]
    kv_got = from_tok(kv_sent, dc=1)[:, rows:]
    mine, others = suffix_attention(core[None], queries, kv, halo, partial, bias, scale)
    got = from_tok(others, dc=1)
    strip_3, mine = lax.optimization_barrier((strip_3, mine))
    strips.append(strip_3)
    strips_other.append(from_tok(strip_3, dc=1))
    projected = output_projection(place_xc, mine, got, strips, strips_other)
    cache = in_core_order(core, kv[:, :rows], kv_got, 2)
    return (projected[None], cache[0][None], cache[1][None])


def solution(mesh):
    return jax.shard_map(
        per_device,
        mesh=mesh,
        in_specs=(
            P("grp", "tok", None),
            P("grp", "tok"),
            P("grp", "tok", None),
            P(),
            P(),
            P(),
            P(),
            P("tok", None),
            P("tok", None),
        ),
        out_specs=(P("grp", "tok", None), P("grp", "tok", None), P("grp", "tok", None)),
        check_vma=False,
    )
```

```python
import functools
import math

import jax
import jax.numpy as jnp
from jax import lax
from jax.experimental import pallas as pl
from jax.experimental.pallas import tpu as pltpu
from jax.sharding import PartitionSpec as P

NX, NZ, NC, NY = 4, 8, 2, 4

epsilon = 1e-06
theta_base = 1000000.0
floor_score = -1e30
VMEM_LIMIT = 56 * 1024 * 1024


def place(x, z, c):
    return (x * NZ + z) * NC + c


def from_tok(block, dx=0, dz=0, dc=0):
    route = [
        (place((x + dx) % NX, (z + dz) % NZ, (c + dc) % NC), place(x, z, c))
        for x in range(NX)
        for z in range(NZ)
        for c in range(NC)
    ]
    return lax.ppermute(block, "tok", route)


def from_grp(block, dy):
    return lax.ppermute(block, "grp", [((y + dy) % NY, y) for y in range(NY)])


def from_previous_chip(block):
    chips = NX * NZ
    route = [(p * NC + c, (p + 1) * NC + c) for p in range(chips - 1) for c in range(NC)]
    return lax.ppermute(block, "tok", route)


def in_core_order(core, mine, other, axis):
    first = jnp.where(core == 0, mine, other)
    second = jnp.where(core == 0, other, mine)
    return jnp.concatenate([first, second], axis=axis)


def norm_kernel(x_ref, own_ref, peer_ref, gain_ref, np_ref, nq_ref, scratch):
    half = own_ref.shape[0]
    gain = gain_ref[...].astype(jnp.float32)
    x = x_ref[0]
    for part, ref in enumerate((own_ref, peer_ref)):
        tokens = ref[...].astype(jnp.float32)
        mean = jnp.mean(tokens * tokens, axis=-1, keepdims=True)
        scratch[...] = (tokens * lax.rsqrt(mean + epsilon) * gain).astype(jnp.bfloat16)
        for j in range(NX):
            at = pl.multiple_of(((x + j) % NX) * 512, 512)
            np_ref[pl.ds(part * half, half), j * 256 : (j + 1) * 256] = scratch[:, pl.ds(at, 256)]
            at = pl.multiple_of(((x + j) % NX) * 512 + 256, 256)
            nq_ref[pl.ds(part * half, half), j * 256 : (j + 1) * 256] = scratch[:, pl.ds(at, 256)]


def input_norm(x, own, peer, gain):
    rows, width = own.shape
    out = jax.ShapeDtypeStruct((2 * rows, width // 2), jnp.bfloat16)
    vmem = pl.BlockSpec(memory_space=pltpu.VMEM)
    return pl.pallas_call(
        norm_kernel,
        out_shape=(out, out),
        in_specs=[pl.BlockSpec(memory_space=pltpu.SMEM), vmem, vmem, vmem],
        out_specs=(vmem, vmem),
        scratch_shapes=[pltpu.VMEM((rows, width), jnp.bfloat16)],
        compiler_params=pltpu.CompilerParams(vmem_limit_bytes=VMEM_LIMIT),
        name="input_norm",
    )(x, own, peer, gain)


def qkv_kernel(
    y_ref, np_ref, nq_ref, p0, p1, p2, p3, q0, q1, q2, q3, cos_ref, sin_ref, qg_ref, kg_ref,
    q_out, kv_out, acc, b1, b2, b3, sems
):
    step = pl.program_id(0)
    block = (y_ref[0] + step) % NY
    copies = [
        pltpu.make_async_copy(p, b, sems.at[i])
        for i, (p, b) in enumerate(((p1, b1), (p2, b2), (p3, b3)))
    ]

    @pl.when(step == 0)
    def _():
        for copy in copies:
            copy.start()

    def dot(a, b):
        return jnp.dot(a, b, preferred_element_type=jnp.float32)

    for k, p in enumerate((p0, b1, b2, b3)):

        @pl.when(step == k)
        def _(p=p, k=k):
            if k > 0:
                copies[k - 1].wait()
            total = dot(np_ref[...], p[...])
            for j, q in enumerate((q0, q1, q2, q3)):
                total = total + dot(nq_ref[:, j * 256 : (j + 1) * 256], q[...])
            acc[...] = total

    def turned(gain_ref, out):
        gain = gain_ref[...].astype(jnp.float32)
        for h in range(2):
            a = acc[:, h * 128 : (h + 1) * 128]
            mean = jnp.mean(a * a, axis=-1, keepdims=True)
            a = a * lax.rsqrt(mean + epsilon) * gain
            a = a * cos_ref[...] + pltpu.roll(a, 64, 1) * sin_ref[...]
            out[0, :, h * 128 : (h + 1) * 128] = a.astype(jnp.bfloat16)

    @pl.when(block < 2)
    def _():
        turned(qg_ref, q_out)

    @pl.when(block == 2)
    def _():
        turned(kg_ref, kv_out)

    @pl.when(block == 3)
    def _():
        kv_out[0] = acc[...].astype(jnp.bfloat16)


def query_block(i, y_ref):
    block = (y_ref[0] + i) % NY
    return jnp.where(block < 2, block, jnp.where(i >= block - 1, 1, 0)), 0, 0


def key_value_block(i, y_ref):
    block = (y_ref[0] + i) % NY
    return jnp.where(block >= 2, block - 2, jnp.where(i >= block + 1, 1, 0)), 0, 0


def joint_projection(y, normed_p, normed_q, p, q, cosine, sine, query_gain, key_gain):
    rows = normed_p.shape[0]
    whole = lambda a: pl.BlockSpec(a.shape, lambda i, y_ref: (0,) * a.ndim)
    args = [normed_p, normed_q, *p, *q, cosine, sine, query_gain, key_gain]
    out = jax.ShapeDtypeStruct((2, rows, 256), jnp.bfloat16)
    return pl.pallas_call(
        qkv_kernel,
        out_shape=(out, out),
        grid_spec=pltpu.PrefetchScalarGridSpec(
            num_scalar_prefetch=1,
            grid=(NY,),
            in_specs=[whole(normed_p), whole(normed_q), whole(p[0])]
            + [pl.BlockSpec(memory_space=pl.ANY)] * 3
            + [pl.BlockSpec((256, 256), lambda i, y_ref: (i, 0))] * 4
            + [whole(a) for a in args[-4:]],
            out_specs=(
                pl.BlockSpec((1, rows, 256), query_block),
                pl.BlockSpec((1, rows, 256), key_value_block),
            ),
            scratch_shapes=[pltpu.VMEM((rows, 256), jnp.float32)]
            + [pltpu.VMEM((1024, 256), jnp.bfloat16)] * 3
            + [pltpu.SemaphoreType.DMA((3,))],
        ),
        compiler_params=pltpu.CompilerParams(
            dimension_semantics=("arbitrary",), vmem_limit_bytes=VMEM_LIMIT
        ),
        cost_estimate=pl.CostEstimate(
            flops=2 * rows * 2048 * 1024, transcendentals=0, bytes_accessed=8 << 20
        ),
        name="joint_projection",
    )(y, *args)


LANES = (((1,), (1,)), ((), ()))


def fold(op, blocks):
    return functools.reduce(
        op, [b[:, i : i + 128] for b in blocks for i in range(0, b.shape[1], 128)]
    )


def row_max(blocks):
    return jnp.max(fold(jnp.maximum, blocks), axis=-1, keepdims=True)


def prefix_kernel(scale, core_ref, q_ref, k_ref, v_ref, acc_ref, stat_ref):
    rows, step = 256, 512
    starts = range(0, k_ref.shape[0], step)
    for r in range(0, q_ref.shape[1], rows):
        for h in range(2):
            q = q_ref[0, r : r + rows, h * 128 : (h + 1) * 128]
            scores = [
                lax.dot_general(
                    q, k_ref[i : i + step, :], LANES, preferred_element_type=jnp.float32
                )
                for i in starts
            ]
            top = row_max(scores)
            total = jnp.zeros(q.shape, jnp.float32)
            acc = jnp.zeros(q.shape, jnp.float32)
            for s, i in zip(scores, starts):
                w = jnp.exp2((s - top) * scale)
                total = total + fold(jnp.add, [w])
                acc = acc + jnp.dot(
                    w.astype(jnp.bfloat16),
                    v_ref[i : i + step, :],
                    preferred_element_type=jnp.float32,
                )
            acc_ref[h, r : r + rows, :] = acc
            stat_ref[h, r : r + rows, 0:1] = top
            stat_ref[h, r : r + rows, 1:2] = jnp.sum(total, axis=-1, keepdims=True)


def prefix_attention(core, qkv, prefix, scale):
    rows = qkv.shape[1]
    keys = prefix.shape[0]
    out = jax.ShapeDtypeStruct((4, rows, 128), jnp.float32)
    pair = pl.BlockSpec((2, rows, 128), lambda g, c: (g, 0, 0))
    return pl.pallas_call(
        functools.partial(prefix_kernel, scale),
        out_shape=(out, out),
        grid_spec=pltpu.PrefetchScalarGridSpec(
            num_scalar_prefetch=1,
            grid=(2,),
            in_specs=[
                pl.BlockSpec((1, rows, 256), lambda g, c: (g, 0, 0)),
                pl.BlockSpec((keys, 128), lambda g, c: (0, 2 * c[0] + g)),
                pl.BlockSpec((keys, 128), lambda g, c: (0, 4 + 2 * c[0] + g)),
            ],
            out_specs=(pair, pair),
        ),
        compiler_params=pltpu.CompilerParams(
            dimension_semantics=("arbitrary",), vmem_limit_bytes=VMEM_LIMIT
        ),
        cost_estimate=pl.CostEstimate(
            flops=4 * 4 * rows * keys * 128, transcendentals=4 * rows * keys, bytes_accessed=4 << 20
        ),
        name="prefix_attention",
    )(core, qkv, prefix, prefix)


def suffix_kernel(
    scale, core_ref, q_ref, ko_ref, vo_ref, kh_ref, vh_ref, acc_ref, stat_ref, bias_ref,
    own_ref, peer_ref
):
    core = core_ref[0]
    rows = own_ref.shape[0]
    zero = pl.ds(pl.multiple_of(core * rows, rows), rows)
    one = pl.ds(pl.multiple_of((1 - core) * rows, rows), rows)
    for r, out_ref in enumerate((own_ref, peer_ref)):
        block = slice(r * rows, (r + 1) * rows)
        third = [jnp.where(core == r, h[0, block, :], o[0, block, :])
                 for h, o in ((kh_ref, ko_ref), (vh_ref, vo_ref))]
        keys = [kh_ref[0, one, :], ko_ref[0, zero, :], third[0]]
        values = [vh_ref[0, one, :], vo_ref[0, zero, :], third[1]]
        for h in range(2):
            q = q_ref[0, block, h * 128 : (h + 1) * 128]
            scores = [
                lax.dot_general(q, k, LANES, preferred_element_type=jnp.float32)
                + bias_ref[r, :, i * rows : (i + 1) * rows].astype(jnp.float32)
                for i, k in enumerate(keys)
            ]
            before = stat_ref[h, block, 0:1]
            top = jnp.maximum(before, row_max(scores))
            shrink = jnp.exp2((before - top) * scale)
            weights = [jnp.exp2((s - top) * scale) for s in scores]
            total = jnp.sum(fold(jnp.add, weights), axis=-1, keepdims=True)
            total = stat_ref[h, block, 1:2] * shrink + total
            acc = acc_ref[h, block, :] * shrink
            for w, v in zip(weights, values):
                acc = acc + jnp.dot(w.astype(jnp.bfloat16), v, preferred_element_type=jnp.float32)
            out_ref[:, h * 128 : (h + 1) * 128] = (acc / total).astype(jnp.bfloat16)


def suffix_attention(core, queries, own, halo, partial, bias, scale):
    rows = queries.shape[1]
    pair = pl.BlockSpec((2, rows, 128), lambda g, c: (g, 0, 0))
    head = lambda block: pl.BlockSpec((1, rows, 128), lambda g, c: (block, 0, g))
    out = jax.ShapeDtypeStruct((rows // 2, 512), jnp.bfloat16)
    out_spec = pl.BlockSpec((rows // 2, 256), lambda g, c: (0, g))
    return pl.pallas_call(
        functools.partial(suffix_kernel, scale),
        out_shape=(out, out),
        grid_spec=pltpu.PrefetchScalarGridSpec(
            num_scalar_prefetch=1,
            grid=(2,),
            in_specs=[
                pl.BlockSpec((1, rows, 256), lambda g, c: (g, 0, 0)),
                head(0),
                head(1),
                head(0),
                head(1),
                pair,
                pair,
                pl.BlockSpec(bias.shape, lambda g, c: (0, 0, 0)),
            ],
            out_specs=(out_spec, out_spec),
        ),
        compiler_params=pltpu.CompilerParams(
            dimension_semantics=("arbitrary",), vmem_limit_bytes=VMEM_LIMIT
        ),
        cost_estimate=pl.CostEstimate(
            flops=4 * 4 * rows * 768 * 128, transcendentals=4 * rows * 768, bytes_accessed=4 << 20
        ),
        name="suffix_attention",
    )(core, queries, own, own, halo, halo, *partial, bias)


def out_kernel(place_ref, mine_ref, other_ref, *refs):
    *weights, out_ref, heads = refs
    x, core = place_ref[0], place_ref[1]
    heads[:, pl.ds(pl.multiple_of(core * 512, 512), 512)] = mine_ref[...]
    heads[:, pl.ds(pl.multiple_of((1 - core) * 512, 512), 512)] = other_ref[...]
    for c, strips in ((core, weights[:NX]), (1 - core, weights[NX:])):
        total = jnp.zeros((mine_ref.shape[0], 1024), jnp.float32)
        for j, strip in enumerate(strips):
            at = pl.multiple_of(((x + j) % NX) * 256, 256)
            total = total + jnp.dot(
                heads[:, pl.ds(at, 256)], strip[...], preferred_element_type=jnp.float32
            )
        out_ref[:, pl.ds(pl.multiple_of(c * 1024, 1024), 1024)] = total.astype(jnp.bfloat16)


def output_projection(place_xc, mine, other, strips, strips_other):
    rows = mine.shape[0]
    vmem = pl.BlockSpec(memory_space=pltpu.VMEM)
    args = [mine, other, *strips, *strips_other]
    return pl.pallas_call(
        out_kernel,
        out_shape=jax.ShapeDtypeStruct((rows, 2048), jnp.bfloat16),
        in_specs=[pl.BlockSpec(memory_space=pltpu.SMEM)] + [vmem] * len(args),
        out_specs=vmem,
        scratch_shapes=[pltpu.VMEM((rows, 1024), jnp.bfloat16)],
        compiler_params=pltpu.CompilerParams(vmem_limit_bytes=VMEM_LIMIT),
        cost_estimate=pl.CostEstimate(
            flops=2 * rows * 1024 * 2048, transcendentals=0, bytes_accessed=6 << 20
        ),
        name="output_projection",
    )(place_xc, *args)


def choose_kernel(y_ref, owner_ref, *refs):
    *owners, out_ref = refs
    steps = (owner_ref[y_ref[0]] - y_ref[0] + NY) % NY
    for k, owner in enumerate(owners):

        @pl.when(steps == k)
        def _(owner=owner):
            for i in range(4):
                out_ref[32 * i : 32 * (i + 1), :] = owner[:, i * 256 : (i + 1) * 256]


def choose(y, prefix_owner, owners):
    vmem = pl.BlockSpec(memory_space=pltpu.VMEM)
    smem = pl.BlockSpec(memory_space=pltpu.SMEM)
    return pl.pallas_call(
        choose_kernel,
        out_shape=jax.ShapeDtypeStruct((128, 256), jnp.bfloat16),
        in_specs=[smem, smem] + [vmem] * NY,
        out_specs=vmem,
        name="choose",
    )(y, prefix_owner, *owners)


GROUP_ZC = [[place(x, z, c) for z in range(NZ) for c in range(NC)] for x in range(NX)]


def per_device(
    hidden_in, doc_ids, prefix_kv, prefix_owner, norm_gain, query_gain, key_norm_gain, w_qkv, w_out
):
    rows = hidden_in.shape[1]
    head_dim = query_gain.shape[0]
    prefix_len = prefix_kv.shape[1] * lax.axis_size("tok")
    scale = head_dim ** (-0.5) * math.log2(math.e)
    place_tok = lax.axis_index("tok")
    y = lax.axis_index("grp")
    x, z, core = place_tok // (NZ * NC), (place_tok // NC) % NZ, place_tok % NC

    own = hidden_in[0]
    out_strip = lax.all_gather(w_out, "tok", axis_index_groups=GROUP_ZC, tiled=True)
    owners = [prefix_kv[0]] + [from_grp(prefix_kv[0], d) for d in range(1, NY)]

    def columns(c):
        start = jnp.where(y < 2, 512 * c + 256 * y, 512 * y + 256 * c)
        return lax.dynamic_slice(w_qkv, (jnp.int32(0), start), (w_qkv.shape[0], 256))

    marks = (doc_ids + 1).astype(jnp.bfloat16)
    first = jnp.concatenate(
        [
            jnp.concatenate([columns(0), columns(1)], axis=1),
            jnp.pad(marks, ((0, 7), (0, 256))),
        ],
        axis=0,
    )
    both = lax.all_gather(first, "tok", axis_index_groups=GROUP_ZC)
    peer = from_tok(own, dc=1)
    both, owners, peer, query_gain, key_norm_gain = lax.optimization_barrier(
        (both, owners, peer, query_gain, key_norm_gain)
    )

    marks_x = both[:, 32, :256]
    strip = lax.dynamic_slice_in_dim(both[:, :32], core * 256, 256, 2).reshape(512, 256)
    prefix_rows = choose(y[None], prefix_owner, owners)
    p_own = jnp.concatenate(
        [strip[:256]]
        + [prefix_rows]
        + [jnp.pad(marks_x[14:], ((0, 6), (0, 0)))]
    )
    q_own = jnp.concatenate([strip[256:], jnp.zeros((8, 256), jnp.bfloat16)])
    p_all = [p_own] + [from_tok(p_own, dx=d) for d in (2, 1, 3)]
    p_all = [p_all[0], p_all[2], p_all[1], p_all[3]]
    q_all = [q_own] + [from_grp(q_own, d) for d in range(1, NY)]
    p_all, q_all = lax.optimization_barrier((p_all, q_all))

    p0 = jnp.concatenate([p[:256] for p in p_all])
    q0 = jnp.concatenate([q[:256] for q in q_all])
    prefix_part = jnp.concatenate(
        [
            jnp.concatenate([p[256 + 32 * i : 288 + 32 * i] for i in range(4)], axis=1)
            for p in p_all
        ]
    )
    p2 = from_grp(p0, 2)
    p1, p3 = from_grp(p0, 1), from_grp(p0, 3)
    q1, q3 = from_tok(q0, dx=1), from_tok(q0, dx=3)
    q2 = from_tok(q0, dx=2)
    prefix = lax.all_gather(prefix_part, "tok", axis_index_groups=GROUP_ZC, tiled=True)

    own, peer, norm_gain, p1 = lax.optimization_barrier((own, peer, norm_gain, p1))
    normed_p, normed_q = input_norm(x[None], own, peer, norm_gain[None, :])
    marks_left = jnp.where(x > 0, p_all[3][384:386], 0)
    near = lax.dynamic_slice_in_dim(
        jnp.concatenate([marks_left, marks_x]).astype(jnp.float32), 2 * z, 4, 0
    )
    row = lax.broadcasted_iota(jnp.int32, (rows, rows), 0)
    column = lax.broadcasted_iota(jnp.int32, (rows, rows), 1)
    bias, offset = [], []
    for part in range(2):
        upper = (core + part) % 2
        marks_q = lax.dynamic_index_in_dim(near, 2 + upper, 0, keepdims=False)[:, None]
        third = jnp.where(upper == 0, near[0], near[3])
        counted = 0
        for keys, whole in ((near[1], True), (near[2], upper == 1), (third, upper == 0)):
            same = marks_q == keys[None, :]
            seen = same & ((column <= row) | whole)
            bias.append(jnp.where(seen, 0.0, floor_score).astype(jnp.bfloat16))
            counted += jnp.sum((same & ((column < row) | whole)).astype(jnp.int32), axis=1)
        offset.append(counted)
    bias = jnp.stack(
        [jnp.concatenate(bias[:3], axis=1), jnp.concatenate(bias[3:], axis=1)]
    )
    offset = jnp.concatenate(offset)
    token_positions = (prefix_len + offset).astype(jnp.float32)
    half_width = head_dim // 2
    freqs = theta_base ** (-jnp.arange(half_width, dtype=jnp.float32) / half_width)
    angles = token_positions[:, None] * freqs[None, :]
    cosine, sine = jnp.cos(angles), jnp.sin(angles)
    cosine = jnp.concatenate([cosine, cosine], axis=1)
    sine = jnp.concatenate([-sine, sine], axis=1)
    gains = (query_gain[None, :], key_norm_gain[None, :])

    under = (normed_p, normed_q, cosine, sine, bias, gains)
    pieces = ([p0, p1, p2, p3], [q0, q1, q2, q3])
    place_xc = jnp.stack([x, core])

    out_mine = lax.dynamic_slice_in_dim(out_strip, core * 1024, 1024, 1)
    out_mine, pieces, under, place_xc = lax.optimization_barrier(
        (out_mine, pieces, under, place_xc)
    )
    normed_p, normed_q, cosine, sine, bias, gains = under
    strip_3 = from_tok(out_mine, dx=3)
    strips = [out_mine] + [from_tok(out_mine, dx=d) for d in (1, 2)]
    queries, kv = joint_projection(y[None], normed_p, normed_q, *pieces, cosine, sine, *gains)
    halo = from_previous_chip(kv)

    partial = prefix_attention(core[None], queries, prefix, scale)
    strips, partial, kv_sent = lax.optimization_barrier((strips, partial, kv))
    strips_other = [from_tok(s, dc=1) for s in strips]
    kv_got = from_tok(kv_sent, dc=1)[:, rows:]
    mine, others = suffix_attention(core[None], queries, kv, halo, partial, bias, scale)
    got = from_tok(others, dc=1)
    strip_3, mine = lax.optimization_barrier((strip_3, mine))
    strips.append(strip_3)
    strips_other.append(from_tok(strip_3, dc=1))
    projected = output_projection(place_xc, mine, got, strips, strips_other)
    cache = in_core_order(core, kv[:, :rows], kv_got, 2)
    return (projected[None], cache[0][None], cache[1][None])


def solution(mesh):
    return jax.shard_map(
        per_device,
        mesh=mesh,
        in_specs=(
            P("grp", "tok", None),
            P("grp", "tok"),
            P("grp", "tok", None),
            P(),
            P(),
            P(),
            P(),
            P("tok", None),
            P("tok", None),
        ),
        out_specs=(P("grp", "tok", None), P("grp", "tok", None), P("grp", "tok", None)),
        check_vma=False,
    )
```
